128 devices in a mesh: col: 32 (over z, y, x_hi), row: 4 (over x_lo, core).
Axes of the slice: x: 4 (x_hi: 2, x_lo: 2; x = x_hi * 2 + x_lo), y: 4, z: 4, core: 2. Of those that a mesh axis runs over, the one named last changes fastest.
Arguments:
- hamiltonian: float32 [16384, 16384], P('row', 'col'), as said below
Outputs:
- reduced: float32 [16384, 16384], P('row', 'col')
Inputs may be any that keep to these rules, and one draw needn't show every extreme that they name: hamiltonian is symmetric.
All inputs are finite; a program needn't handle non-finite values.
Results may differ from the reference program's by a relative error of at most 0.00019.
Values sent between devices are 32-bit elements; how exact they have to be, the bound alone decides.
No kernel may reach another device: no remote copies, remote signals or barrier semaphores. Data moves between devices by JAX's collectives and lax.ppermute only.
A program may use at most 128 MiB of HBM per device.

```python
import jax
import jax.numpy as jnp
from jax import lax

M = 16384
NB = 256
PANELS = 2


def draw_hamiltonian(key, part):
    first_key = jax.random.fold_in(jax.random.fold_in(key, 11), 0)
    noise = jax.random.normal(first_key, (M, M), jnp.float32)
    sym = (noise + noise.T) * 0.7071
    return sym


def setup_inputs(seed: int = 0) -> dict:
    streams_of = jax.random.split(jax.random.key(seed), 2)
    return {
        "hamiltonian": draw_hamiltonian(jax.random.fold_in(streams_of[1], 71), 0),
    }


def product(left, right):
    return jnp.dot(left.astype(jnp.float32), right.astype(jnp.float32), precision=lax.Precision.HIGHEST, preferred_element_type=jnp.float32)

def inner_tn(left, right):
    return lax.dot_general(left.astype(jnp.float32), right.astype(jnp.float32), (((0,), (0,)), ((), ())), precision=lax.Precision.HIGHEST, preferred_element_type=jnp.float32)

def outer_nt(left, right):
    return lax.dot_general(left.astype(jnp.float32), right.astype(jnp.float32), (((1,), (1,)), ((), ())), precision=lax.Precision.HIGHEST, preferred_element_type=jnp.float32)

def normalize(panel):
    gram = inner_tn(panel, panel)
    lower = jnp.linalg.cholesky(gram)
    return lax.linalg.triangular_solve(lower, panel, left_side=False, lower=True, transpose_a=True)

def coupling_of(top_rows):
    square = jnp.eye(NB, dtype=top_rows.dtype) - top_rows.T
    normal_eq = inner_tn(square, square)
    factor = jnp.linalg.cholesky(normal_eq)
    middle = lax.linalg.triangular_solve(factor, square.T, left_side=True, lower=True)
    return lax.linalg.triangular_solve(factor, middle, left_side=True, lower=True, transpose_a=True)

def reduce_panel(matrix, first_col):
    first_row = first_col + NB
    row_ids = jnp.arange(M, dtype=jnp.int32)
    live = (row_ids >= first_row)[:, None]
    panel = jnp.where(live, matrix[:, first_col:first_col + NB], jnp.zeros((), matrix.dtype))
    basis = normalize(panel)
    coupling = coupling_of(basis[first_row:first_row + NB])
    ident = (row_ids[:, None] - first_row == jnp.arange(NB, dtype=jnp.int32)[None, :]).astype(matrix.dtype)
    vectors = ident - basis
    applied = product(product(matrix, vectors), coupling)
    inner = product(coupling.T, inner_tn(vectors, applied))
    shifted = applied - 0.5 * product(vectors, inner)
    return matrix - outer_nt(vectors, shifted) - outer_nt(shifted, vectors)

def reference(hamiltonian):
    matrix = hamiltonian
    for panel_index in range(PANELS):
        matrix = reduce_panel(matrix, panel_index * NB)
    return matrix
```

```python
import jax
import jax.numpy as jnp
from jax import lax
from jax.experimental import pallas as pl
from jax.experimental.pallas import tpu as pltpu
from jax.sharding import Mesh, PartitionSpec as P

NB = 256
PIECE = 128
COL = ("z", "y", "xh")
ROW = ("xl", "c")
F32 = jnp.float32


def contract(left, right, dims, precision=lax.Precision.HIGHEST):
    return lax.dot_general(
        left, right, (dims, ((), ())), precision=precision, preferred_element_type=F32
    )


def nn(left, right):
    return contract(left, right, ((1,), (0,)))


def tn(left, right):
    return contract(left, right, ((0,), (0,)))


def nt(left, right):
    return contract(left, right, ((1,), (1,)))


def ring(block, axis, shift):
    return lax.ppermute(block, axis, [(k, (k + shift) % 4) for k in range(4)])


def swap(block, axis):
    return lax.ppermute(block, axis, [(0, 1), (1, 0)])


def row_sum(stacked):
    half = stacked.shape[0] // 2
    core = lax.axis_index("c")
    low, high = stacked[:half], stacked[half:]
    mine = jnp.where(core == 0, low, high) + swap(jnp.where(core == 0, high, low), "c")
    mine = mine + swap(mine, "xl")
    other = swap(mine, "c")
    return jnp.concatenate(
        [jnp.where(core == 0, mine, other), jnp.where(core == 0, other, mine)], 0
    )


def gather_rows(piece):
    z, y, xh = (lax.axis_index(a) for a in COL)
    other = swap(piece, "xh")
    pair = jnp.concatenate(
        [jnp.where(xh == 0, piece, other), jnp.where(xh == 0, other, piece)], 0
    )
    out = jnp.zeros((4, 4, 2 * PIECE, NB), F32)
    for half, (first, second) in enumerate((("y", "z"), ("z", "y"))):
        at_first, at_second = (y, z) if half == 0 else (z, y)
        own = pair[:, half * 128 : (half + 1) * 128]
        left, right = ring(own, first, 1), ring(own, first, 3)
        far = jnp.concatenate(
            [ring(left[:PIECE], first, 1), ring(right[PIECE:], first, 3)], 0
        )
        line = jnp.zeros((4, 2 * PIECE, 128), F32)
        for shift, block in ((0, own), (-1, left), (1, right), (2, far)):
            line = lax.dynamic_update_slice(line, block[None], ((at_first + shift) % 4, 0, 0))
        left, right = ring(line, second, 1), ring(line, second, 3)
        far = jnp.concatenate([ring(left[:2], second, 1), ring(right[2:], second, 3)], 0)
        for shift, block in ((0, line), (-1, left), (1, right), (2, far)):
            place = (at_second + shift) % 4
            if half == 0:
                out = lax.dynamic_update_slice(out, block[None], (place, 0, 0, 0))
            else:
                out = lax.dynamic_update_slice(out, block[:, None], (0, place, 0, 128))
    return out.reshape(32 * PIECE, NB)


def reduce_pieces(partial):
    xl, core = lax.axis_index("xl"), lax.axis_index("c")
    half = 2 * PIECE
    low, high = partial[:half], partial[half:]
    mine = jnp.where(core == 0, low, high) + swap(jnp.where(core == 0, high, low), "c")
    piece = 0.0
    for k in range(2):
        part = lax.dynamic_slice_in_dim(mine, ((xl + k) % 2) * PIECE, PIECE, 0)
        perm = [
            ((z * 2 + l) * 2 + c, (2 * c + (l + k) % 2) * 4 + z)
            for z in range(4)
            for l in range(2)
            for c in range(2)
        ]
        piece = piece + lax.ppermute(part, ("z", "xl", "c"), perm)
    mine = mine + swap(mine, "xl")
    other = swap(mine, "c")
    whole = jnp.concatenate(
        [jnp.where(core == 0, mine, other), jnp.where(core == 0, other, mine)], 0
    )
    return whole, piece


def scatter_pieces(block):
    piece = 0.0
    for q in range(4):
        perm = [(z * 4, q * 4 + z) for z in range(4)]
        piece = piece + lax.ppermute(
            block[q * PIECE : (q + 1) * PIECE], ("z", "xl", "c"), perm
        )
    return piece


def row_broadcast(block):
    first = lax.axis_index(ROW) == 0
    block = jnp.where(first, block, 0.0)
    block = block + swap(block, "xl")
    return block + swap(block, "c")


BF16 = jnp.bfloat16


def split(block):
    high = block.astype(BF16)
    return high, (block - high.astype(F32)).astype(BF16)


def split_outside(block):
    high = lax.reduce_precision(block, 8, 7)
    return high.astype(BF16), (block - high).astype(BF16)


def dot3(left, right):
    (lh, ll), (rh, rl) = left, right

    def dot(a, b):
        return jnp.dot(a, b, preferred_element_type=F32)

    return dot(lh, rh) + (dot(lh, rl) + dot(ll, rh))


def whole(shape):
    return pl.BlockSpec(shape, lambda b: (0,) * len(shape))


NATURAL = pl.BlockSpec((512, 512), lambda b: (b, 0))
GATHERED = pl.BlockSpec((4, 1, PIECE, NB), lambda b: (0, b, 0, 0))
GATHERED_SHAPE = jax.ShapeDtypeStruct((4, 8, PIECE, NB), F32)
SQUARE = jax.ShapeDtypeStruct((NB, NB), F32)
LARGE = pltpu.CompilerParams(vmem_limit_bytes=48 << 20)


def rows_of(ref):
    return ref[...].reshape(512, NB)


def blocks_of(array):
    return array.reshape(4, 8, PIECE, NB)


def product_kernel(m_ref, b_ref, out_ref, acc_ref):
    step = pl.program_id(0)

    @pl.when(step == 0)
    def _():
        acc_ref[...] = jnp.zeros_like(acc_ref)

    acc_ref[...] += dot3(split(rows_of(b_ref).T), split(m_ref[...]))

    @pl.when(step == pl.num_programs(0) - 1)
    def _():
        out_ref[...] = acc_ref[...].T


def product_of(matrix, base):
    return pl.pallas_call(
        product_kernel,
        grid=(8,),
        in_specs=[NATURAL, GATHERED],
        out_specs=whole((512, NB)),
        out_shape=jax.ShapeDtypeStruct((512, NB), F32),
        scratch_shapes=[pltpu.VMEM((NB, 512), F32)],
        compiler_params=LARGE,
        name="product",
    )(matrix, blocks_of(base))


def image_kernel(e_ref, w_ref, v_ref, h_ref, l_ref, out_ref, inner_ref):
    step = pl.program_id(0)

    @pl.when(step == 0)
    def _():
        inner_ref[...] = jnp.zeros_like(inner_ref)

    image = rows_of(e_ref) - dot3(split(rows_of(w_ref)), (h_ref[...], l_ref[...]))
    out_ref[...] = image.reshape(out_ref.shape)
    inner_ref[...] += dot3(split(image.T), split(rows_of(v_ref)))


def image_of(cols, product, vectors, inv):
    high, low = split_outside(inv.T)
    image, inner = pl.pallas_call(
        image_kernel,
        grid=(8,),
        in_specs=[GATHERED, GATHERED, GATHERED, whole((NB, NB)), whole((NB, NB))],
        out_specs=[GATHERED, whole((NB, NB))],
        out_shape=[GATHERED_SHAPE, SQUARE],
        compiler_params=LARGE,
        name="image",
    )(blocks_of(cols), blocks_of(product), blocks_of(vectors), high, low)
    return image.reshape(4096, NB), inner


def second_kernel(r_ref, e_ref, i_ref, v_ref, h_ref, l_ref, m_ref, base_ref, gram_ref, cross_ref, prod_ref, acc_ref):
    step = pl.program_id(0)

    @pl.when(step == 0)
    def _():
        gram_ref[...] = jnp.zeros_like(gram_ref)
        cross_ref[...] = jnp.zeros_like(cross_ref)
        acc_ref[...] = jnp.zeros_like(acc_ref)

    left = [split(rows_of(i_ref)), split(rows_of(v_ref))]
    base = rows_of(e_ref)
    for k in range(2):
        at = slice(k * NB, (k + 1) * NB)
        base = base - dot3(left[k], (h_ref[at, :], l_ref[at, :]))
    base = jnp.where((r_ref[0] == 0) & (step == 0), 0.0, base)
    base_ref[...] = base.reshape(base_ref.shape)
    turned = base.T
    parts = split(turned)
    gram_ref[...] += nn(turned, base)
    for k in range(2):
        cross_ref[:, k * NB : (k + 1) * NB] += dot3(parts, left[k])
    acc_ref[...] += dot3(parts, split(m_ref[...]))

    @pl.when(step == pl.num_programs(0) - 1)
    def _():
        prod_ref[...] = acc_ref[...].T


def second_of(row, cols, image, vectors, right, matrix):
    high, low = split_outside(right)
    base, gram, cross, product = pl.pallas_call(
        second_kernel,
        grid=(8,),
        in_specs=[
            pl.BlockSpec(memory_space=pltpu.SMEM),
            GATHERED,
            GATHERED,
            GATHERED,
            whole((2 * NB, NB)),
            whole((2 * NB, NB)),
            NATURAL,
        ],
        out_specs=[GATHERED, whole((NB, NB)), whole((NB, 2 * NB)), whole((512, NB))],
        out_shape=[
            GATHERED_SHAPE,
            SQUARE,
            jax.ShapeDtypeStruct((NB, 2 * NB), F32),
            jax.ShapeDtypeStruct((512, NB), F32),
        ],
        scratch_shapes=[pltpu.VMEM((NB, 512), F32)],
        compiler_params=LARGE,
        name="second",
    )(row[None], blocks_of(cols), blocks_of(image), blocks_of(vectors), high, low, matrix)
    return base.reshape(4096, NB), gram, cross, product


def update_kernel(m_ref, i_ref, v_ref, h_ref, l_ref, out_ref):
    out = m_ref[...]
    for k, ref in enumerate((i_ref, v_ref)):
        at = slice(k * NB, (k + 1) * NB)
        out = out - dot3(split(rows_of(ref)), (h_ref[at, :], l_ref[at, :]))
    out_ref[...] = out


def update_of(matrix, image, vectors, right):
    high, low = split_outside(right)
    return pl.pallas_call(
        update_kernel,
        grid=(8,),
        in_specs=[NATURAL, GATHERED, GATHERED, whole((512, 512)), whole((512, 512))],
        out_specs=NATURAL,
        out_shape=jax.ShapeDtypeStruct((4096, 512), F32),
        compiler_params=LARGE,
        name="update",
    )(matrix, blocks_of(image), blocks_of(vectors), high, low)


def diagonal_inverse(block, size):
    rows = lax.broadcasted_iota(jnp.int32, (size, 128), 0)
    lanes = lax.broadcasted_iota(jnp.int32, (size, 128), 1)
    work = jnp.where(lanes < size, block, (lanes - size == rows).astype(F32))
    for k in range(size - 1):
        pivot = work[k : k + 1, :]
        factor = work[:, k : k + 1] / pivot[:, k : k + 1]
        work = work - jnp.where(rows > k, factor, 0.0) * pivot
    diag = jnp.sum(jnp.where(lanes == rows, work, 0.0), axis=1, keepdims=True)
    return (work / jnp.sqrt(diag))[:, size : 2 * size]


def invert_factor(m_ref, x_ref, size=32):
    rows = lax.broadcasted_iota(jnp.int32, (NB, NB), 0)
    x_ref[...] = (rows == lax.broadcasted_iota(jnp.int32, (NB, NB), 1)).astype(F32)
    lane = lax.broadcasted_iota(jnp.int32, (size, NB), 1)
    for at in range(0, NB, size):
        strip = m_ref[at : at + size, :]
        block = strip[:, at // 128 * 128 : at // 128 * 128 + 128]
        if at % 128:
            block = pltpu.roll(block, 128 - at % 128, 1)
        inv = diagonal_inverse(block, size)
        strip = jnp.where(lane >= at, nn(inv, strip), 0.0)
        solved = nn(inv, x_ref[at : at + size, :])
        below = at + size
        if below < NB:
            left = strip.T[below:]
            m_ref[below:, :] -= nn(left, strip)
            x_ref[below:, :] -= nn(left, solved)
        x_ref[at : at + size, :] = solved


def factor_kernel(g_ref, inv_ref, m_ref):
    m_ref[...] = g_ref[...]
    invert_factor(m_ref, inv_ref)


def inverse_factor(gram):
    return pl.pallas_call(
        factor_kernel,
        out_shape=SQUARE,
        scratch_shapes=[pltpu.VMEM((NB, NB), F32)],
        name="factor",
    )(gram)


def coupling_kernel(t_ref, inv_ref, top_ref, out_ref, m_ref, f_ref):
    rows = lax.broadcasted_iota(jnp.int32, (NB, NB), 0)
    eye = (rows == lax.broadcasted_iota(jnp.int32, (NB, NB), 1)).astype(F32)
    top = eye - nt(t_ref[...], inv_ref[...])
    top_ref[...] = top
    m_ref[...] = nt(top, top)
    invert_factor(m_ref, f_ref)
    factor = f_ref[...]
    out_ref[...] = nn(factor.T, nn(factor, top))


def coupling_of(base_top, inv):
    return pl.pallas_call(
        coupling_kernel,
        out_shape=(SQUARE, SQUARE),
        scratch_shapes=[pltpu.VMEM((NB, NB), F32)] * 2,
        name="coupling",
    )(base_top, inv)


def shards(matrix):
    z, y, xh = (lax.axis_index(a) for a in COL)
    row = lax.axis_index(ROW)
    on_first = row == 0
    lanes = jnp.arange(NB, dtype=jnp.int32)[None, :]

    where_in = jnp.arange(32 * PIECE, dtype=jnp.int32)
    gathered_rows = (
        row * 4096
        + (where_in // 256 % 4 * 2 + where_in // 128 % 2) * 512
        + where_in // 1024 * 128
        + where_in % 128
    )[:, None]
    column_rows = (((z * 4 + y) * 2 + xh) * 512 + jnp.arange(512, dtype=jnp.int32))[:, None]
    piece_rows = (
        row * 4096 + (y * 2 + xh) * 512 + z * 128 + jnp.arange(128, dtype=jnp.int32)
    )[:, None]

    def unit(rows, first):
        return (rows - first == lanes).astype(F32)

    def rows_at(block, first):
        cube = block.reshape(4, 8, PIECE, NB)
        at = first // 512
        q = first % 512 // 128
        return jnp.where(on_first, jnp.concatenate([cube[q, at], cube[q + 1, at]], 0), 0.0)

    def high(dims, left, right):
        return contract(left, right, dims, lax.Precision.HIGH)

    wide_nt = ((1,), (1,))

    strip = matrix[: 3 * NB].T
    pieces = scatter_pieces(strip[:, : 2 * NB])
    base_piece = jnp.where(piece_rows >= NB, pieces[:, :NB], 0.0)
    next_piece = pieces[:, NB:]
    next_cols = lax.all_gather(next_piece, COL, tiled=True)
    base = gather_rows(base_piece)
    strip, base = lax.optimization_barrier((strip, base))

    product_j, product_p = reduce_pieces(product_of(matrix, base))
    stat = row_sum(
        jnp.concatenate([tn(base, base), rows_at(base, 256), rows_at(base, 512)], 0)
    )
    product = gather_rows(product_p)
    last_piece = scatter_pieces(strip[:, 2 * NB :])
    strip = row_broadcast(strip)
    inv = inverse_factor(stat[:256])
    top, coupling = coupling_of(stat[256:512], inv)
    top_next = -nt(stat[512:768], inv)
    vectors = unit(gathered_rows, 256) - high(wide_nt, base, inv)

    image, inner = image_of(next_cols, product, vectors, inv)
    stat = row_sum(jnp.concatenate([inner, rows_at(image, 256), rows_at(image, 512)], 0))
    inner = nn(tn(coupling, stat[:256]), coupling)
    image_top, image_next = stat[256:512], stat[512:]

    def factors(vec, img):
        return nt(coupling, vec), tn(coupling, img.T) - nt(inner, vec)

    right = jnp.concatenate(factors(top, image_top), 0)
    base2, gram, cross, partial = second_of(row, next_cols, image, vectors, right, matrix)
    stat = row_sum(jnp.concatenate([gram, rows_at(base2, 512)], 0))
    product_j2, product_p2 = reduce_pieces(partial)
    cross = row_sum(cross.T)
    inv2 = inverse_factor(stat[:256])
    mix_v = tn(coupling, cross[:256]) - nn(inner, cross[256:])
    mix_i = nn(coupling, cross[256:])
    next_a, next_b = factors(top_next, image_next)

    def second_image(cols, base_rows, first, prod1, prod2, rows):
        vec = unit(rows, 256) - nt(base_rows, inv)
        img = first - nt(prod1, inv)
        prod = prod2 - nn(vec, mix_v) - nn(img, mix_i)
        return vec, img, cols - nn(img, next_a) - nn(vec, next_b) - nt(prod, inv2)

    image2_p = second_image(last_piece, base_piece, next_piece, product_p, product_p2, piece_rows)[2]
    image2 = gather_rows(image2_p)

    base_j = jnp.where(column_rows >= 256, strip[:, :256], 0.0)
    vectors_j, image_j, image2_j = second_image(
        strip[:, 512:], base_j, strip[:, 256:512], product_j, product_j2, column_rows
    )
    top2, coupling2 = coupling_of(stat[256:], inv2)
    base2_j = jnp.where(
        column_rows >= 512,
        strip[:, 256:512] - nn(image_j, right[:256]) - nn(vectors_j, right[256:]),
        0.0,
    )
    vectors2 = unit(gathered_rows, 512) - high(wide_nt, base2, inv2)
    vectors2_j = unit(column_rows, 512) - nt(base2_j, inv2)
    first = update_of(
        matrix, image, vectors, jnp.concatenate(factors(vectors_j, image_j), 0)
    )

    inner2 = row_sum(high(((0,), (0,)), vectors2, image2))
    inner2 = nn(tn(coupling2, inner2), coupling2)
    last = jnp.concatenate(
        [nt(coupling2, vectors2_j), tn(coupling2, image2_j.T) - nt(inner2, vectors2_j)], 0
    )
    return update_of(first, image2, vectors2, last)


def solution(mesh):
    fine = Mesh(mesh.devices.reshape(4, 4, 2, 2, 2), COL + ROW)
    return jax.shard_map(
        shards,
        mesh=fine,
        in_specs=(P(ROW, COL),),
        out_specs=P(ROW, COL),
        check_vma=False,
    )
```

```python
import jax
import jax.numpy as jnp
from jax import lax
from jax.experimental import pallas as pl
from jax.experimental.pallas import tpu as pltpu
from jax.sharding import Mesh, PartitionSpec as P

NB = 256
PIECE = 128
COL = ("z", "y", "xh")
ROW = ("xl", "c")
F32 = jnp.float32


def contract(left, right, dims, precision=lax.Precision.HIGHEST):
    return lax.dot_general(
        left, right, (dims, ((), ())), precision=precision, preferred_element_type=F32
    )


def nn(left, right):
    return contract(left, right, ((1,), (0,)))


def tn(left, right):
    return contract(left, right, ((0,), (0,)))


def nt(left, right):
    return contract(left, right, ((1,), (1,)))


def ring(block, axis, shift):
    return lax.ppermute(block, axis, [(k, (k + shift) % 4) for k in range(4)])


def swap(block, axis):
    return lax.ppermute(block, axis, [(0, 1), (1, 0)])


def row_sum(stacked):
    half = stacked.shape[0] // 2
    core = lax.axis_index("c")
    low, high = stacked[:half], stacked[half:]
    mine = jnp.where(core == 0, low, high) + swap(jnp.where(core == 0, high, low), "c")
    mine = mine + swap(mine, "xl")
    other = swap(mine, "c")
    return jnp.concatenate(
        [jnp.where(core == 0, mine, other), jnp.where(core == 0, other, mine)], 0
    )


def gather_rows(pair):
    z, y = lax.axis_index("z"), lax.axis_index("y")
    out = jnp.zeros((4, 4, 2 * PIECE, NB), F32)
    for half, (first, second) in enumerate((("y", "z"), ("z", "y"))):
        at_first, at_second = (y, z) if half == 0 else (z, y)
        own = pair[:, half * 128 : (half + 1) * 128]
        left, right, far = ring(own, first, 1), ring(own, first, 3), ring(own, first, 2)
        line = jnp.zeros((4, 2 * PIECE, 128), F32)
        for shift, block in ((0, own), (-1, left), (1, right), (2, far)):
            line = lax.dynamic_update_slice(line, block[None], ((at_first + shift) % 4, 0, 0))
        left, right = ring(line, second, 1), ring(line, second, 3)
        far = jnp.concatenate([ring(left[:2], second, 1), ring(right[2:], second, 3)], 0)
        for shift, block in ((0, line), (-1, left), (1, right), (2, far)):
            place = (at_second + shift) % 4
            if half == 0:
                out = lax.dynamic_update_slice(out, block[None], (place, 0, 0, 0))
            else:
                out = lax.dynamic_update_slice(out, block[:, None], (0, place, 0, 128))
    return out.reshape(32 * PIECE, NB)


def reduce_pieces(partial):
    xl, core = lax.axis_index("xl"), lax.axis_index("c")
    half = 2 * PIECE
    low, high = partial[:half], partial[half:]
    mine = jnp.where(core == 0, low, high) + swap(jnp.where(core == 0, high, low), "c")
    piece = 0.0
    for k in range(2):
        part = lax.dynamic_slice_in_dim(mine, ((xl + k) % 2) * PIECE, PIECE, 0)
        perm = [
            ((z * 2 + l) * 2 + c, (2 * c + (l + k) % 2) * 4 + z)
            for z in range(4)
            for l in range(2)
            for c in range(2)
        ]
        piece = piece + lax.ppermute(part, ("z", "xl", "c"), perm)
    mine = mine + swap(mine, "xl")
    other = swap(mine, "c")
    whole = jnp.concatenate(
        [jnp.where(core == 0, mine, other), jnp.where(core == 0, other, mine)], 0
    )
    return whole, piece


def scatter_pieces(block):
    piece = 0.0
    for q in range(4):
        perm = [(z * 4, q * 4 + z) for z in range(4)]
        piece = piece + lax.ppermute(
            block[q * PIECE : (q + 1) * PIECE], ("z", "xl", "c"), perm
        )
    return piece


def row_broadcast(block):
    first = lax.axis_index(ROW) == 0
    block = jnp.where(first, block, 0.0)
    block = block + swap(block, "xl")
    return block + swap(block, "c")


def pair_up(piece):
    xh = lax.axis_index("xh")
    other = swap(piece, "xh")
    return jnp.concatenate(
        [jnp.where(xh == 0, piece, other), jnp.where(xh == 0, other, piece)], 0
    )


def gather_pairs(pair):
    return lax.all_gather(pair, ("z", "y"), tiled=True)


def column_sum(block):
    block = block + swap(block, "xh")
    for axis in ("y", "z"):
        for step in (1, 2):
            block = block + lax.ppermute(block, axis, [(k, k ^ step) for k in range(4)])
    return block


BF16 = jnp.bfloat16


def split(block):
    high = block.astype(BF16)
    return high, (block - high.astype(F32)).astype(BF16)


def split_outside(block):
    high = lax.reduce_precision(block, 8, 7)
    return high.astype(BF16), (block - high).astype(BF16)


def dot3(left, right):
    (lh, ll), (rh, rl) = left, right

    def dot(a, b):
        return jnp.dot(a, b, preferred_element_type=F32)

    return dot(lh, rh) + (dot(lh, rl) + dot(ll, rh))


def whole(shape):
    return pl.BlockSpec(shape, lambda b: (0,) * len(shape))


NATURAL = pl.BlockSpec((512, 512), lambda b: (b, 0))
GATHERED = pl.BlockSpec((4, 1, PIECE, NB), lambda b: (0, b, 0, 0))
GATHERED_SHAPE = jax.ShapeDtypeStruct((4, 8, PIECE, NB), F32)
SQUARE = jax.ShapeDtypeStruct((NB, NB), F32)
LARGE = pltpu.CompilerParams(vmem_limit_bytes=48 << 20)


def rows_of(ref):
    return ref[...].reshape(512, NB)


def blocks_of(array):
    return array.reshape(4, 8, PIECE, NB)


def product_kernel(m_ref, b_ref, out_ref, acc_ref):
    step = pl.program_id(0)

    @pl.when(step == 0)
    def _():
        acc_ref[...] = jnp.zeros_like(acc_ref)

    acc_ref[...] += dot3(split(rows_of(b_ref).T), split(m_ref[...]))

    @pl.when(step == pl.num_programs(0) - 1)
    def _():
        out_ref[...] = acc_ref[...].T


def product_of(matrix, base):
    return pl.pallas_call(
        product_kernel,
        grid=(8,),
        in_specs=[NATURAL, GATHERED],
        out_specs=whole((512, NB)),
        out_shape=jax.ShapeDtypeStruct((512, NB), F32),
        scratch_shapes=[pltpu.VMEM((NB, 512), F32)],
        compiler_params=LARGE,
        name="product",
    )(matrix, blocks_of(base))


def image_kernel(e_ref, w_ref, v_ref, h_ref, l_ref, out_ref, inner_ref):
    step = pl.program_id(0)

    @pl.when(step == 0)
    def _():
        inner_ref[...] = jnp.zeros_like(inner_ref)

    image = rows_of(e_ref) - dot3(split(rows_of(w_ref)), (h_ref[...], l_ref[...]))
    out_ref[...] = image.reshape(out_ref.shape)
    inner_ref[...] += dot3(split(image.T), split(rows_of(v_ref)))


def image_of(cols, product, vectors, inv):
    high, low = split_outside(inv.T)
    image, inner = pl.pallas_call(
        image_kernel,
        grid=(8,),
        in_specs=[GATHERED, GATHERED, GATHERED, whole((NB, NB)), whole((NB, NB))],
        out_specs=[GATHERED, whole((NB, NB))],
        out_shape=[GATHERED_SHAPE, SQUARE],
        compiler_params=LARGE,
        name="image",
    )(blocks_of(cols), blocks_of(product), blocks_of(vectors), high, low)
    return image.reshape(4096, NB), inner


def second_kernel(r_ref, e_ref, i_ref, v_ref, h_ref, l_ref, m_ref, base_ref, gram_ref, cross_ref, prod_ref, acc_ref):
    step = pl.program_id(0)

    @pl.when(step == 0)
    def _():
        gram_ref[...] = jnp.zeros_like(gram_ref)
        cross_ref[...] = jnp.zeros_like(cross_ref)
        acc_ref[...] = jnp.zeros_like(acc_ref)

    left = [split(rows_of(i_ref)), split(rows_of(v_ref))]
    base = rows_of(e_ref)
    for k in range(2):
        at = slice(k * NB, (k + 1) * NB)
        base = base - dot3(left[k], (h_ref[at, :], l_ref[at, :]))
    base = jnp.where((r_ref[0] == 0) & (step == 0), 0.0, base)
    base_ref[...] = base.reshape(base_ref.shape)
    turned = base.T
    parts = split(turned)
    gram_ref[...] += nn(turned, base)
    for k in range(2):
        cross_ref[:, k * NB : (k + 1) * NB] += dot3(parts, left[k])
    acc_ref[...] += dot3(parts, split(m_ref[...]))

    @pl.when(step == pl.num_programs(0) - 1)
    def _():
        prod_ref[...] = acc_ref[...].T


def second_of(row, cols, image, vectors, right, matrix):
    high, low = split_outside(right)
    base, gram, cross, product = pl.pallas_call(
        second_kernel,
        grid=(8,),
        in_specs=[
            pl.BlockSpec(memory_space=pltpu.SMEM),
            GATHERED,
            GATHERED,
            GATHERED,
            whole((2 * NB, NB)),
            whole((2 * NB, NB)),
            NATURAL,
        ],
        out_specs=[GATHERED, whole((NB, NB)), whole((NB, 2 * NB)), whole((512, NB))],
        out_shape=[
            GATHERED_SHAPE,
            SQUARE,
            jax.ShapeDtypeStruct((NB, 2 * NB), F32),
            jax.ShapeDtypeStruct((512, NB), F32),
        ],
        scratch_shapes=[pltpu.VMEM((NB, 512), F32)],
        compiler_params=LARGE,
        name="second",
    )(row[None], blocks_of(cols), blocks_of(image), blocks_of(vectors), high, low, matrix)
    return base.reshape(4096, NB), gram, cross, product


def update_kernel(m_ref, h_ref, l_ref, *refs):
    out = m_ref[...]
    for k, ref in enumerate(refs[:-1]):
        at = slice(k * NB, (k + 1) * NB)
        out = out - dot3(split(rows_of(ref)), (h_ref[at, :], l_ref[at, :]))
    refs[-1][...] = out


def update_of(matrix, lefts, right):
    high, low = split_outside(right)
    return pl.pallas_call(
        update_kernel,
        grid=(8,),
        in_specs=[NATURAL, whole(right.shape), whole(right.shape)] + [GATHERED] * len(lefts),
        out_specs=NATURAL,
        out_shape=jax.ShapeDtypeStruct((4096, 512), F32),
        compiler_params=LARGE,
        name="update",
    )(matrix, high, low, *(blocks_of(left) for left in lefts))


def diagonal_inverse(block, size):
    rows = lax.broadcasted_iota(jnp.int32, (size, 128), 0)
    lanes = lax.broadcasted_iota(jnp.int32, (size, 128), 1)
    work = jnp.where(lanes < size, block, (lanes - size == rows).astype(F32))
    count = size // 8
    groups = [work[8 * i : 8 * i + 8] for i in range(count)]
    place = rows[:8]

    def spread(tile, t):
        return jnp.broadcast_to(tile[t : t + 1, :], (8, 128))

    for a in range(count):
        columns = [
            [jnp.broadcast_to(groups[i][:, k : k + 1], (8, 128)) for k in range(8 * a, 8 * a + 8)]
            for i in range(a, count)
        ]
        for t in range(8):
            if a == count - 1 and t == 7:
                break
            scale = 1.0 / spread(columns[0][t], t)
            row = spread(groups[a], t)
            heads = [spread(columns[0][u], t) for u in range(t + 1, 8)]
            for i in range(a, count):
                own = columns[i - a]
                factor = own[t] * scale
                if i == a:
                    if t == 7:
                        continue
                    factor = jnp.where(place > t, factor, 0.0)
                groups[i] = groups[i] - factor * row
                for u in range(t + 1, 8):
                    own[u] = own[u] - factor * heads[u - t - 1]
    work = jnp.concatenate(groups, 0)
    diag = jnp.sum(jnp.where(lanes == rows, work, 0.0), axis=1, keepdims=True)
    return (work / jnp.sqrt(diag))[:, size : 2 * size]


def invert_factor(m_ref, x_ref, size=64):
    rows = lax.broadcasted_iota(jnp.int32, (NB, NB), 0)
    x_ref[...] = (rows == lax.broadcasted_iota(jnp.int32, (NB, NB), 1)).astype(F32)
    lane = lax.broadcasted_iota(jnp.int32, (size, NB), 1)
    for at in range(0, NB, size):
        strip = m_ref[at : at + size, :]
        block = strip[:, at // 128 * 128 : at // 128 * 128 + 128]
        if at % 128:
            block = pltpu.roll(block, 128 - at % 128, 1)
        inv = diagonal_inverse(block, size)
        strip = jnp.where(lane >= at, nn(inv, strip), 0.0)
        solved = nn(inv, x_ref[at : at + size, :])
        below = at + size
        if below < NB:
            left = strip.T[below:]
            m_ref[below:, :] -= nn(left, strip)
            x_ref[below:, :] -= nn(left, solved)
        x_ref[at : at + size, :] = solved


def factor_kernel(g_ref, inv_ref, m_ref):
    m_ref[...] = g_ref[...]
    invert_factor(m_ref, inv_ref)


def inverse_factor(gram):
    return pl.pallas_call(
        factor_kernel,
        out_shape=SQUARE,
        scratch_shapes=[pltpu.VMEM((NB, NB), F32)],
        name="factor",
    )(gram)


def coupling_kernel(t_ref, inv_ref, top_ref, out_ref, m_ref, f_ref):
    rows = lax.broadcasted_iota(jnp.int32, (NB, NB), 0)
    eye = (rows == lax.broadcasted_iota(jnp.int32, (NB, NB), 1)).astype(F32)
    top = eye - nt(t_ref[...], inv_ref[...])
    top_ref[...] = top
    m_ref[...] = nt(top, top)
    invert_factor(m_ref, f_ref)
    factor = f_ref[...]
    out_ref[...] = nn(factor.T, nn(factor, top))


def coupling_of(base_top, inv):
    return pl.pallas_call(
        coupling_kernel,
        out_shape=(SQUARE, SQUARE),
        scratch_shapes=[pltpu.VMEM((NB, NB), F32)] * 2,
        name="coupling",
    )(base_top, inv)


def shards(matrix):
    z, y, xh = (lax.axis_index(a) for a in COL)
    row = lax.axis_index(ROW)
    on_first = row == 0
    lanes = jnp.arange(NB, dtype=jnp.int32)[None, :]

    where_in = jnp.arange(32 * PIECE, dtype=jnp.int32)
    gathered_rows = (
        row * 4096
        + (where_in // 256 % 4 * 2 + where_in // 128 % 2) * 512
        + where_in // 1024 * 128
        + where_in % 128
    )[:, None]
    column_rows = (((z * 4 + y) * 2 + xh) * 512 + jnp.arange(512, dtype=jnp.int32))[:, None]
    piece_rows = (
        row * 4096 + (y * 2 + xh) * 512 + z * 128 + jnp.arange(128, dtype=jnp.int32)
    )[:, None]

    def unit(rows, first):
        return (rows - first == lanes).astype(F32)

    def rows_at(block, first):
        cube = block.reshape(4, 8, PIECE, NB)
        at = first // 512
        q = first % 512 // 128
        return jnp.where(on_first, jnp.concatenate([cube[q, at], cube[q + 1, at]], 0), 0.0)

    def high(dims, left, right):
        return contract(left, right, dims, lax.Precision.HIGH)

    wide_nt = ((1,), (1,))

    strip = matrix[: 3 * NB].T
    pieces = scatter_pieces(strip[:, : 2 * NB])
    base_piece = jnp.where(piece_rows >= NB, pieces[:, :NB], 0.0)
    next_piece = pieces[:, NB:]
    pairs = pair_up(jnp.concatenate([base_piece, next_piece], 1))
    next_cols = gather_pairs(pairs[:, NB:])
    strip, pairs = lax.optimization_barrier((strip, pairs))
    last_piece = scatter_pieces(strip[:, 2 * NB :])
    strip = row_broadcast(strip)
    base = gather_rows(pairs[:, :NB])

    product_j, product_p = reduce_pieces(product_of(matrix, base))
    stat = row_sum(
        jnp.concatenate([tn(base, base), rows_at(base, 256), rows_at(base, 512)], 0)
    )
    product = gather_pairs(pair_up(product_p))
    inv = inverse_factor(stat[:256])
    top, coupling = coupling_of(stat[256:512], inv)
    top_next = -nt(stat[512:768], inv)
    vectors = unit(gathered_rows, 256) - high(wide_nt, base, inv)

    image, inner = image_of(next_cols, product, vectors, inv)
    stat = row_sum(jnp.concatenate([inner, rows_at(image, 256), rows_at(image, 512)], 0))
    inner = nn(tn(coupling, stat[:256]), coupling)
    image_top, image_next = stat[256:512], stat[512:]

    def factors(vec, img):
        return nt(coupling, vec), tn(coupling, img.T) - nt(inner, vec)

    right = jnp.concatenate(factors(top, image_top), 0)
    base2, gram, cross, partial = second_of(row, next_cols, image, vectors, right, matrix)
    stat = row_sum(jnp.concatenate([gram, rows_at(base2, 512)], 0))
    product_j2, product_p2 = reduce_pieces(partial)
    cross = row_sum(cross.T)
    inv2 = inverse_factor(stat[:256])
    mix_v = tn(coupling, cross[:256]) - nn(inner, cross[256:])
    mix_i = nn(coupling, cross[256:])
    next_a, next_b = factors(top_next, image_next)

    def second_image(cols, base_rows, first, prod1, prod2, rows):
        vec = unit(rows, 256) - nt(base_rows, inv)
        img = first - nt(prod1, inv)
        prod = prod2 - nn(vec, mix_v) - nn(img, mix_i)
        return vec, img, cols - nn(img, next_a) - nn(vec, next_b) - nt(prod, inv2)

    image2_p = second_image(last_piece, base_piece, next_piece, product_p, product_p2, piece_rows)[2]
    image2 = gather_pairs(pair_up(image2_p))

    base_j = jnp.where(column_rows >= 256, strip[:, :256], 0.0)
    vectors_j, image_j, image2_j = second_image(
        strip[:, 512:], base_j, strip[:, 256:512], product_j, product_j2, column_rows
    )
    top2, coupling2 = coupling_of(stat[256:], inv2)
    base2_j = jnp.where(
        column_rows >= 512,
        strip[:, 256:512] - nn(image_j, right[:256]) - nn(vectors_j, right[256:]),
        0.0,
    )
    vectors2 = unit(gathered_rows, 512) - high(wide_nt, base2, inv2)
    vectors2_j = unit(column_rows, 512) - nt(base2_j, inv2)
    first = update_of(
        matrix, (image, vectors), jnp.concatenate(factors(vectors_j, image_j), 0)
    )
    quarter = lax.dynamic_slice_in_dim(tn(vectors2_j, image2_j), row * 64, 64, 0)
    inner2 = lax.all_gather(column_sum(quarter), ROW, tiled=True)
    inner2 = nn(tn(coupling2, inner2), coupling2)
    last_b = tn(coupling2, image2_j.T) - nt(inner2, vectors2_j)
    first = update_of(first, (vectors2,), last_b)
    first, image2 = lax.optimization_barrier((first, image2))
    return update_of(first, (image2,), nt(coupling2, vectors2_j))


def solution(mesh):
    fine = Mesh(mesh.devices.reshape(4, 4, 2, 2, 2), COL + ROW)
    return jax.shard_map(
        shards,
        mesh=fine,
        in_specs=(P(ROW, COL),),
        out_specs=P(ROW, COL),
        check_vma=False,
    )
```

```python
import jax
import jax.numpy as jnp
from jax import lax
from jax.experimental import pallas as pl
from jax.experimental.pallas import tpu as pltpu
from jax.sharding import Mesh, PartitionSpec as P

NB = 256
PIECE = 128
COL = ("z", "y", "xh")
ROW = ("xl", "c")
F32 = jnp.float32


def contract(left, right, dims, precision=lax.Precision.HIGHEST):
    return lax.dot_general(
        left, right, (dims, ((), ())), precision=precision, preferred_element_type=F32
    )


def nn(left, right):
    return contract(left, right, ((1,), (0,)))


def tn(left, right):
    return contract(left, right, ((0,), (0,)))


def nt(left, right):
    return contract(left, right, ((1,), (1,)))


def ring(block, axis, shift):
    return lax.ppermute(block, axis, [(k, (k + shift) % 4) for k in range(4)])


def swap(block, axis):
    return lax.ppermute(block, axis, [(0, 1), (1, 0)])


def core_half(stacked):
    half = stacked.shape[0] // 2
    core = lax.axis_index("c")
    low, high = stacked[:half], stacked[half:]
    return jnp.where(core == 0, low, high) + swap(jnp.where(core == 0, high, low), "c")


def both_halves(mine):
    core = lax.axis_index("c")
    other = swap(mine, "c")
    return jnp.concatenate(
        [jnp.where(core == 0, mine, other), jnp.where(core == 0, other, mine)], 0
    )


def row_sum(stacked):
    mine = core_half(stacked)
    return both_halves(mine + swap(mine, "xl"))


def gather_rows(pair):
    z, y = lax.axis_index("z"), lax.axis_index("y")
    out = jnp.zeros((4, 4, 2 * PIECE, NB), F32)
    for half, (first, second) in enumerate((("y", "z"), ("z", "y"))):
        at_first, at_second = (y, z) if half == 0 else (z, y)
        own = pair[:, half * 128 : (half + 1) * 128]
        left, right, far = ring(own, first, 1), ring(own, first, 3), ring(own, first, 2)
        line = jnp.zeros((4, 2 * PIECE, 128), F32)
        for shift, block in ((0, own), (-1, left), (1, right), (2, far)):
            line = lax.dynamic_update_slice(line, block[None], ((at_first + shift) % 4, 0, 0))
        left, right = ring(line, second, 1), ring(line, second, 3)
        far = jnp.concatenate([ring(left[:2], second, 1), ring(right[2:], second, 3)], 0)
        for shift, block in ((0, line), (-1, left), (1, right), (2, far)):
            place = (at_second + shift) % 4
            if half == 0:
                out = lax.dynamic_update_slice(out, block[None], (place, 0, 0, 0))
            else:
                out = lax.dynamic_update_slice(out, block[:, None], (0, place, 0, 128))
    return out.reshape(32 * PIECE, NB)


def piece_of(mine):
    xl = lax.axis_index("xl")
    piece = 0.0
    for k in range(2):
        part = lax.dynamic_slice_in_dim(mine, ((xl + k) % 2) * PIECE, PIECE, 0)
        perm = [
            ((z * 2 + l) * 2 + c, (2 * c + (l + k) % 2) * 4 + z)
            for z in range(4)
            for l in range(2)
            for c in range(2)
        ]
        piece = piece + lax.ppermute(part, ("z", "xl", "c"), perm)
    return piece


def scatter_pieces(half):
    piece = 0.0
    for k in range(2):
        perm = [(z * 4 + c, (2 * c + k) * 4 + z) for z in range(4) for c in range(2)]
        piece = piece + lax.ppermute(
            half[k * PIECE : (k + 1) * PIECE], ("z", "xl", "c"), perm
        )
    return piece


def pair_up(piece):
    xh = lax.axis_index("xh")
    other = swap(piece, "xh")
    return jnp.concatenate(
        [jnp.where(xh == 0, piece, other), jnp.where(xh == 0, other, piece)], 0
    )


def gather_pairs(pair):
    return lax.all_gather(pair, ("z", "y"), tiled=True)


def axis_sum(block, axis):
    return (block + ring(block, axis, 2)) + (ring(block, axis, 1) + ring(block, axis, 3))


BF16 = jnp.bfloat16


def split(block):
    high = block.astype(BF16)
    return high, (block - high.astype(F32)).astype(BF16)


def split_outside(block):
    high = lax.reduce_precision(block, 8, 7)
    return high.astype(BF16), (block - high).astype(BF16)


def dot3(left, right):
    (lh, ll), (rh, rl) = left, right

    def dot(a, b):
        return jnp.dot(a, b, preferred_element_type=F32)

    return dot(lh, rh) + (dot(lh, rl) + dot(ll, rh))


def whole(shape):
    return pl.BlockSpec(shape, lambda b: (0,) * len(shape))


NATURAL = pl.BlockSpec((512, 512), lambda b: (b, 0))
GATHERED = pl.BlockSpec((4, 1, PIECE, NB), lambda b: (0, b, 0, 0))
GATHERED_SHAPE = jax.ShapeDtypeStruct((4, 8, PIECE, NB), F32)
SQUARE = jax.ShapeDtypeStruct((NB, NB), F32)
LARGE = pltpu.CompilerParams(vmem_limit_bytes=48 << 20)


def cost(us):
    return pl.CostEstimate(flops=us * 10**9, bytes_accessed=us << 20, transcendentals=0)


def rows_of(ref):
    return ref[...].reshape(512, NB)


def blocks_of(array):
    return array.reshape(4, 8, PIECE, NB)


def product_kernel(m_ref, b_ref, out_ref, gram_ref, acc_ref):
    step = pl.program_id(0)

    @pl.when(step == 0)
    def _():
        acc_ref[...] = jnp.zeros_like(acc_ref)
        gram_ref[...] = jnp.zeros_like(gram_ref)

    base = rows_of(b_ref)
    turned = base.T
    acc_ref[...] += dot3(split(turned), split(m_ref[...]))
    gram_ref[...] += nn(turned, base)

    @pl.when(step == pl.num_programs(0) - 1)
    def _():
        out_ref[...] = acc_ref[...].T


def product_of(matrix, base):
    return pl.pallas_call(
        product_kernel,
        grid=(8,),
        in_specs=[NATURAL, GATHERED],
        out_specs=[whole((512, NB)), whole((NB, NB))],
        out_shape=[jax.ShapeDtypeStruct((512, NB), F32), SQUARE],
        scratch_shapes=[pltpu.VMEM((NB, 512), F32)],
        compiler_params=LARGE,
        cost_estimate=cost(13),
        name="product",
    )(matrix, blocks_of(base))


def image_kernel(e_ref, w_ref, v_ref, h_ref, l_ref, out_ref, inner_ref):
    step = pl.program_id(0)

    @pl.when(step == 0)
    def _():
        inner_ref[...] = jnp.zeros_like(inner_ref)

    image = rows_of(e_ref) - dot3(split(rows_of(w_ref)), (h_ref[...], l_ref[...]))
    out_ref[...] = image.reshape(out_ref.shape)
    inner_ref[...] += dot3(split(image.T), split(rows_of(v_ref)))


def image_of(cols, product, vectors, inv):
    high, low = split_outside(inv.T)
    image, inner = pl.pallas_call(
        image_kernel,
        grid=(8,),
        in_specs=[GATHERED, GATHERED, GATHERED, whole((NB, NB)), whole((NB, NB))],
        out_specs=[GATHERED, whole((NB, NB))],
        out_shape=[GATHERED_SHAPE, SQUARE],
        compiler_params=LARGE,
        cost_estimate=cost(11),
        name="image",
    )(blocks_of(cols), blocks_of(product), blocks_of(vectors), high, low)
    return image.reshape(4096, NB), inner


def second_kernel(r_ref, e_ref, i_ref, v_ref, h_ref, l_ref, m_ref, base_ref, gram_ref, cross_ref, prod_ref, acc_ref):
    step = pl.program_id(0)

    @pl.when(step == 0)
    def _():
        gram_ref[...] = jnp.zeros_like(gram_ref)
        cross_ref[...] = jnp.zeros_like(cross_ref)
        acc_ref[...] = jnp.zeros_like(acc_ref)

    left = [split(rows_of(i_ref)), split(rows_of(v_ref))]
    base = rows_of(e_ref)
    for k in range(2):
        at = slice(k * NB, (k + 1) * NB)
        base = base - dot3(left[k], (h_ref[at, :], l_ref[at, :]))
    base = jnp.where((r_ref[0] == 0) & (step == 0), 0.0, base)
    base_ref[...] = base.reshape(base_ref.shape)
    turned = base.T
    parts = split(turned)
    gram_ref[...] += nn(turned, base)
    for k in range(2):
        cross_ref[:, k * NB : (k + 1) * NB] += dot3(parts, left[k])
    acc_ref[...] += dot3(parts, split(m_ref[...]))

    @pl.when(step == pl.num_programs(0) - 1)
    def _():
        prod_ref[...] = acc_ref[...].T


def second_of(row, cols, image, vectors, right, matrix):
    high, low = split_outside(right)
    base, gram, cross, product = pl.pallas_call(
        second_kernel,
        grid=(8,),
        in_specs=[
            pl.BlockSpec(memory_space=pltpu.SMEM),
            GATHERED,
            GATHERED,
            GATHERED,
            whole((2 * NB, NB)),
            whole((2 * NB, NB)),
            NATURAL,
        ],
        out_specs=[GATHERED, whole((NB, NB)), whole((NB, 2 * NB)), whole((512, NB))],
        out_shape=[
            GATHERED_SHAPE,
            SQUARE,
            jax.ShapeDtypeStruct((NB, 2 * NB), F32),
            jax.ShapeDtypeStruct((512, NB), F32),
        ],
        scratch_shapes=[pltpu.VMEM((NB, 512), F32)],
        compiler_params=LARGE,
        cost_estimate=cost(18),
        name="second",
    )(row[None], blocks_of(cols), blocks_of(image), blocks_of(vectors), high, low, matrix)
    return base.reshape(4096, NB), gram, cross, product


def update_kernel(m_ref, r_ref, *refs):
    parts = [split(rows_of(ref)) for ref in refs[:-1]]
    tops = [top for top, _ in parts]
    left = jnp.concatenate(tops + tops + [rest for _, rest in parts], 1)
    refs[-1][...] = m_ref[...] - jnp.dot(left, r_ref[...], preferred_element_type=F32)


def update_of(matrix, lefts, right):
    top, rest = split_outside(right)
    stack = jnp.concatenate([top, rest, top], 0)
    return pl.pallas_call(
        update_kernel,
        grid=(8,),
        in_specs=[NATURAL, whole(stack.shape)] + [GATHERED] * len(lefts),
        out_specs=NATURAL,
        out_shape=jax.ShapeDtypeStruct((4096, 512), F32),
        compiler_params=LARGE,
        cost_estimate=cost(7 + 3 * len(lefts)),
        name="update",
    )(matrix, stack, *(blocks_of(left) for left in lefts))


def diagonal_inverse(block, size):
    rows = lax.broadcasted_iota(jnp.int32, (size, 128), 0)
    lanes = lax.broadcasted_iota(jnp.int32, (size, 128), 1)
    work = jnp.where(lanes < size, block, (lanes - size == rows).astype(F32))
    count = size // 8
    groups = [work[8 * i : 8 * i + 8] for i in range(count)]
    place = rows[:8]

    def spread(tile, t):
        return jnp.broadcast_to(tile[t : t + 1, :], (8, 128))

    for a in range(count):
        columns = [
            [jnp.broadcast_to(groups[i][:, k : k + 1], (8, 128)) for k in range(8 * a, 8 * a + 8)]
            for i in range(a, count)
        ]
        for t in range(8):
            if a == count - 1 and t == 7:
                break
            scale = 1.0 / spread(columns[0][t], t)
            row = spread(groups[a], t)
            heads = [spread(columns[0][u], t) for u in range(t + 1, 8)]
            for i in range(a, count):
                own = columns[i - a]
                factor = own[t] * scale
                if i == a:
                    if t == 7:
                        continue
                    factor = jnp.where(place > t, factor, 0.0)
                groups[i] = groups[i] - factor * row
                for u in range(t + 1, 8):
                    own[u] = own[u] - factor * heads[u - t - 1]
    work = jnp.concatenate(groups, 0)
    diag = jnp.sum(jnp.where(lanes == rows, work, 0.0), axis=1, keepdims=True)
    return (work / jnp.sqrt(diag))[:, size : 2 * size]


def invert_factor(m_ref, x_ref, size=64):
    rows = lax.broadcasted_iota(jnp.int32, (NB, NB), 0)
    x_ref[...] = (rows == lax.broadcasted_iota(jnp.int32, (NB, NB), 1)).astype(F32)
    lane = lax.broadcasted_iota(jnp.int32, (size, NB), 1)
    for at in range(0, NB, size):
        strip = m_ref[at : at + size, :]
        block = strip[:, at // 128 * 128 : at // 128 * 128 + 128]
        if at % 128:
            block = pltpu.roll(block, 128 - at % 128, 1)
        inv = diagonal_inverse(block, size)
        strip = jnp.where(lane >= at, nn(inv, strip), 0.0)
        solved = nn(inv, x_ref[at : at + size, :])
        below = at + size
        if below < NB:
            left = strip.T[below:]
            m_ref[below:, :] -= nn(left, strip)
            x_ref[below:, :] -= nn(left, solved)
        x_ref[at : at + size, :] = solved


def factor_kernel(g_ref, inv_ref, m_ref):
    m_ref[...] = g_ref[...]
    invert_factor(m_ref, inv_ref)


def inverse_factor(gram):
    return pl.pallas_call(
        factor_kernel,
        out_shape=SQUARE,
        scratch_shapes=[pltpu.VMEM((NB, NB), F32)],
        cost_estimate=cost(12),
        name="factor",
    )(gram)


def coupling_kernel(t_ref, inv_ref, top_ref, out_ref, m_ref, f_ref):
    rows = lax.broadcasted_iota(jnp.int32, (NB, NB), 0)
    eye = (rows == lax.broadcasted_iota(jnp.int32, (NB, NB), 1)).astype(F32)
    top = eye - nt(t_ref[...], inv_ref[...])
    top_ref[...] = top
    m_ref[...] = nt(top, top)
    invert_factor(m_ref, f_ref)
    factor = f_ref[...]
    out_ref[...] = nn(factor.T, nn(factor, top))


def coupling_of(base_top, inv):
    return pl.pallas_call(
        coupling_kernel,
        out_shape=(SQUARE, SQUARE),
        scratch_shapes=[pltpu.VMEM((NB, NB), F32)] * 2,
        cost_estimate=cost(14),
        name="coupling",
    )(base_top, inv)


def shards(matrix):
    z, y, xh = (lax.axis_index(a) for a in COL)
    row = lax.axis_index(ROW)
    on_first = row == 0
    lanes = jnp.arange(NB, dtype=jnp.int32)[None, :]

    where_in = jnp.arange(32 * PIECE, dtype=jnp.int32)
    gathered_rows = (
        row * 4096
        + (where_in // 256 % 4 * 2 + where_in // 128 % 2) * 512
        + where_in // 1024 * 128
        + where_in % 128
    )[:, None]
    column_rows = (((z * 4 + y) * 2 + xh) * 512 + jnp.arange(512, dtype=jnp.int32))[:, None]
    piece_rows = (
        row * 4096 + (y * 2 + xh) * 512 + z * 128 + jnp.arange(128, dtype=jnp.int32)
    )[:, None]

    def unit(rows, first):
        return (rows - first == lanes).astype(F32)

    def rows_at(block, first):
        cube = block.reshape(4, 8, PIECE, NB)
        at = first // 512
        q = first % 512 // 128
        return jnp.where(on_first, jnp.concatenate([cube[q, at], cube[q + 1, at]], 0), 0.0)

    def high(dims, left, right):
        return contract(left, right, dims, lax.Precision.HIGH)

    wide_nt, wide_nn = ((1,), (1,)), ((1,), (0,))

    strip = core_half(jnp.where(on_first, matrix[: 3 * NB].T, 0.0))
    pieces = scatter_pieces(strip[:, : 2 * NB])
    base_piece, next_piece = jnp.where(piece_rows >= NB, pieces[:, :NB], 0.0), pieces[:, NB:]
    next_cols = lax.all_gather(next_piece, COL, tiled=True)
    base = gather_rows(pair_up(base_piece))

    partial, gram = product_of(matrix, base)
    half = core_half(partial)
    product_p = piece_of(half)
    stat = jnp.concatenate([gram, rows_at(base, 256), rows_at(base, 512)], 0)
    product_p, stat, half = lax.optimization_barrier((product_p, stat, half))
    pair, next_cols = lax.optimization_barrier((pair_up(product_p), next_cols))
    product = gather_pairs(pair)
    stat = row_sum(stat)
    product_j = both_halves(half + swap(half, "xl"))
    stat, strip = lax.optimization_barrier((stat, strip))
    inv, last_piece, link = lax.optimization_barrier(
        (inverse_factor(stat[:256]), scatter_pieces(strip[:, 2 * NB :]), swap(strip, "xl"))
    )
    strip = both_halves(strip + link)
    vectors = unit(gathered_rows, 256) - high(wide_nt, base, inv)
    def side(rows, base_rows, first_rows, prod):
        return (
            unit(rows, 256) - high(wide_nt, base_rows, inv),
            first_rows - high(wide_nt, prod, inv),
        )

    product, vectors_p, image_p = lax.optimization_barrier(
        (product, *side(piece_rows, base_piece, next_piece, product_p))
    )
    image, inner = image_of(next_cols, product, vectors, inv)
    base_tops = stat[256:]
    stat = core_half(jnp.concatenate([inner, rows_at(image, 256), rows_at(image, 512)], 0))
    stat, base_tops = lax.optimization_barrier((stat, base_tops))
    top_next = -nt(base_tops[256:], inv)
    link, (top, coupling) = lax.optimization_barrier(
        (swap(stat, "xl"), coupling_of(base_tops[:256], inv))
    )
    stat = both_halves(stat + link)
    inner = nn(tn(coupling, stat[:256]), coupling)
    image_top, image_next = stat[256:512], stat[512:]

    def factors(vec, img):
        return nt(coupling, vec), tn(coupling, img.T) - nt(inner, vec)

    right = jnp.concatenate(factors(top, image_top), 0)
    base2, gram, cross, partial = second_of(row, next_cols, image, vectors, right, matrix)
    stat, half, cross = (
        core_half(v)
        for v in (jnp.concatenate([gram, rows_at(base2, 512)], 0), partial, cross.T)
    )
    next_a, next_b = factors(top_next, image_next)
    cols_p = last_piece - high(wide_nn, image_p, next_a) - high(wide_nn, vectors_p, next_b)
    first_j = strip[:, 256:512]
    vectors_j, image_j = side(
        column_rows, jnp.where(column_rows >= 256, strip[:, :256], 0.0), first_j, product_j
    )
    cols_j = strip[:, 512:] - high(wide_nn, image_j, next_a) - high(wide_nn, vectors_j, next_b)
    base2_j = jnp.where(
        column_rows >= 512,
        first_j - high(wide_nn, image_j, right[:256]) - high(wide_nn, vectors_j, right[256:]),
        0.0,
    )
    stat, half, cross, cols_p, cols_j, base2_j = lax.optimization_barrier(
        (stat + swap(stat, "xl"), half, cross, cols_p, cols_j, base2_j)
    )
    stat = both_halves(stat)
    product_p2, product_j2, cross = piece_of(half), half + swap(half, "xl"), cross + swap(cross, "xl")
    inv2, product_p2, product_j2, cross = lax.optimization_barrier(
        (inverse_factor(stat[:256]), product_p2, product_j2, cross)
    )
    product_j2, cross = both_halves(product_j2), both_halves(cross)
    mix_v = tn(coupling, cross[:256]) - nn(inner, cross[256:])
    mix_i = nn(coupling, cross[256:])
    def second_image(cols, vec, img, prod):
        prod = prod - high(wide_nn, vec, mix_v) - high(wide_nn, img, mix_i)
        return cols - high(wide_nt, prod, inv2)

    image2 = gather_pairs(pair_up(second_image(cols_p, vectors_p, image_p, product_p2)))
    image2_j = second_image(cols_j, vectors_j, image_j, product_j2)
    vectors2_j = unit(column_rows, 512) - high(wide_nt, base2_j, inv2)

    part = lax.dynamic_slice_in_dim(tn(vectors2_j, image2_j), row * 64, 64, 0)
    part = part + swap(part, "xh")
    part, (top2, coupling2) = lax.optimization_barrier((part, coupling_of(stat[256:], inv2)))
    part = axis_sum(part, "y")
    vectors2 = unit(gathered_rows, 512) - high(wide_nt, base2, inv2)
    part, vectors2 = lax.optimization_barrier((part, vectors2))
    inner2 = lax.all_gather(axis_sum(part, "z"), ROW, tiled=True)
    inner2 = nn(tn(coupling2, inner2), coupling2)
    last_a = nt(coupling2, vectors2_j)
    last_b = tn(coupling2, image2_j.T) - nt(inner2, vectors2_j)
    first_a, first_b = factors(vectors_j, image_j)
    right = jnp.concatenate([first_a, first_b, last_b, last_a], 0)
    return update_of(matrix, (image, vectors, vectors2, image2), right)


def solution(mesh):
    fine = Mesh(mesh.devices.reshape(4, 4, 2, 2, 2), COL + ROW)
    return jax.shard_map(
        shards,
        mesh=fine,
        in_specs=(P(ROW, COL),),
        out_specs=P(ROW, COL),
        check_vma=False,
    )
```

```python
import jax
import jax.numpy as jnp
from jax import lax
from jax.experimental import pallas as pl
from jax.experimental.pallas import tpu as pltpu
from jax.sharding import Mesh, PartitionSpec as P

NB = 256
PIECE = 128
COL = ("z", "y", "xh")
ROW = ("xl", "c")
F32 = jnp.float32


def contract(left, right, dims, precision=lax.Precision.HIGHEST):
    return lax.dot_general(
        left, right, (dims, ((), ())), precision=precision, preferred_element_type=F32
    )


def nn(left, right):
    return contract(left, right, ((1,), (0,)))


def tn(left, right):
    return contract(left, right, ((0,), (0,)))


def nt(left, right):
    return contract(left, right, ((1,), (1,)))


def ring(block, axis, shift):
    return lax.ppermute(block, axis, [(k, (k + shift) % 4) for k in range(4)])


def swap(block, axis):
    return lax.ppermute(block, axis, [(0, 1), (1, 0)])


def core_half(stacked):
    half = stacked.shape[0] // 2
    core = lax.axis_index("c")
    low, high = stacked[:half], stacked[half:]
    return jnp.where(core == 0, low, high) + swap(jnp.where(core == 0, high, low), "c")


def both_halves(mine):
    core = lax.axis_index("c")
    other = swap(mine, "c")
    return jnp.concatenate(
        [jnp.where(core == 0, mine, other), jnp.where(core == 0, other, mine)], 0
    )


def row_sum(stacked):
    mine = core_half(stacked)
    return both_halves(mine + swap(mine, "xl"))


def gather_rows(pair):
    z, y = lax.axis_index("z"), lax.axis_index("y")
    out = jnp.zeros((4, 4, 2 * PIECE, NB), F32)
    for half, (first, second) in enumerate((("y", "z"), ("z", "y"))):
        at_first, at_second = (y, z) if half == 0 else (z, y)
        own = pair[:, half * 128 : (half + 1) * 128]
        left, right, far = ring(own, first, 1), ring(own, first, 3), ring(own, first, 2)
        line = jnp.zeros((4, 2 * PIECE, 128), F32)
        for shift, block in ((0, own), (-1, left), (1, right), (2, far)):
            line = lax.dynamic_update_slice(line, block[None], ((at_first + shift) % 4, 0, 0))
        left, right = ring(line, second, 1), ring(line, second, 3)
        far = jnp.concatenate([ring(left[:2], second, 1), ring(right[2:], second, 3)], 0)
        for shift, block in ((0, line), (-1, left), (1, right), (2, far)):
            place = (at_second + shift) % 4
            if half == 0:
                out = lax.dynamic_update_slice(out, block[None], (place, 0, 0, 0))
            else:
                out = lax.dynamic_update_slice(out, block[:, None], (0, place, 0, 128))
    return out.reshape(32 * PIECE, NB)


def piece_of(mine):
    xl = lax.axis_index("xl")
    piece = 0.0
    for k in range(2):
        part = lax.dynamic_slice_in_dim(mine, ((xl + k) % 2) * PIECE, PIECE, 0)
        perm = [
            ((z * 2 + l) * 2 + c, (2 * c + (l + k) % 2) * 4 + z)
            for z in range(4)
            for l in range(2)
            for c in range(2)
        ]
        piece = piece + lax.ppermute(part, ("z", "xl", "c"), perm)
    return piece


def scatter_pieces(half):
    piece = 0.0
    for k in range(2):
        perm = [(z * 4 + c, (2 * c + k) * 4 + z) for z in range(4) for c in range(2)]
        piece = piece + lax.ppermute(
            half[k * PIECE : (k + 1) * PIECE], ("z", "xl", "c"), perm
        )
    return piece


def pair_up(piece):
    xh = lax.axis_index("xh")
    other = swap(piece, "xh")
    return jnp.concatenate(
        [jnp.where(xh == 0, piece, other), jnp.where(xh == 0, other, piece)], 0
    )


def gather_pairs(pair):
    return lax.all_gather(pair, ("z", "y"), tiled=True)


def axis_sum(block, axis):
    return (block + ring(block, axis, 2)) + (ring(block, axis, 1) + ring(block, axis, 3))


BF16 = jnp.bfloat16


def split(block):
    high = block.astype(BF16)
    return high, (block - high.astype(F32)).astype(BF16)


def split_outside(block):
    high = lax.reduce_precision(block, 8, 7)
    return high.astype(BF16), (block - high).astype(BF16)


def dot3(left, right):
    (lh, ll), (rh, rl) = left, right

    def dot(a, b):
        return jnp.dot(a, b, preferred_element_type=F32)

    return dot(lh, rh) + (dot(lh, rl) + dot(ll, rh))


def whole(shape):
    return pl.BlockSpec(shape, lambda b: (0,) * len(shape))


NATURAL = pl.BlockSpec((1024, 512), lambda b: (b, 0))
GATHERED = pl.BlockSpec((4, 2, PIECE, NB), lambda b: (0, b, 0, 0))
GATHERED_SHAPE = jax.ShapeDtypeStruct((4, 8, PIECE, NB), F32)
SQUARE = jax.ShapeDtypeStruct((NB, NB), F32)
LARGE = pltpu.CompilerParams(vmem_limit_bytes=48 << 20)


def cost(us):
    return pl.CostEstimate(flops=us * 10**9, bytes_accessed=us << 20, transcendentals=0)


def rows_of(ref):
    return jnp.concatenate([ref[:, k].reshape(512, NB) for k in range(2)], 0)


def put_rows(ref, rows):
    for k in range(2):
        ref[:, k] = rows[k * 512 : (k + 1) * 512].reshape(4, PIECE, NB)


def blocks_of(array):
    return array.reshape(4, 8, PIECE, NB)


def product_kernel(m_ref, b_ref, out_ref, gram_ref, acc_ref):
    step = pl.program_id(0)

    @pl.when(step == 0)
    def _():
        acc_ref[...] = jnp.zeros_like(acc_ref)
        gram_ref[...] = jnp.zeros_like(gram_ref)

    base = rows_of(b_ref)
    turned = base.T
    acc_ref[...] += dot3(split(turned), split(m_ref[...]))
    gram_ref[...] += nn(turned, base)

    @pl.when(step == pl.num_programs(0) - 1)
    def _():
        out_ref[...] = acc_ref[...].T


def product_of(matrix, base):
    return pl.pallas_call(
        product_kernel,
        grid=(4,),
        in_specs=[NATURAL, GATHERED],
        out_specs=[whole((512, NB)), whole((NB, NB))],
        out_shape=[jax.ShapeDtypeStruct((512, NB), F32), SQUARE],
        scratch_shapes=[pltpu.VMEM((NB, 512), F32)],
        compiler_params=LARGE,
        cost_estimate=cost(13),
        name="product",
    )(matrix, blocks_of(base))


def image_kernel(e_ref, w_ref, v_ref, h_ref, l_ref, out_ref, inner_ref):
    step = pl.program_id(0)

    @pl.when(step == 0)
    def _():
        inner_ref[...] = jnp.zeros_like(inner_ref)

    image = rows_of(e_ref) - dot3(split(rows_of(w_ref)), (h_ref[...], l_ref[...]))
    put_rows(out_ref, image)
    inner_ref[...] += dot3(split(image.T), split(rows_of(v_ref)))


def image_of(cols, product, vectors, inv):
    high, low = split_outside(inv.T)
    image, inner = pl.pallas_call(
        image_kernel,
        grid=(4,),
        in_specs=[GATHERED, GATHERED, GATHERED, whole((NB, NB)), whole((NB, NB))],
        out_specs=[GATHERED, whole((NB, NB))],
        out_shape=[GATHERED_SHAPE, SQUARE],
        compiler_params=LARGE,
        cost_estimate=cost(11),
        name="image",
    )(blocks_of(cols), blocks_of(product), blocks_of(vectors), high, low)
    return image.reshape(4096, NB), inner


def second_kernel(r_ref, e_ref, i_ref, v_ref, h_ref, l_ref, m_ref, base_ref, gram_ref, cross_ref, prod_ref, acc_ref, turn_ref):
    step = pl.program_id(0)

    @pl.when(step == 0)
    def _():
        gram_ref[...] = jnp.zeros_like(gram_ref)
        turn_ref[...] = jnp.zeros_like(turn_ref)
        acc_ref[...] = jnp.zeros_like(acc_ref)

    left = [split(rows_of(i_ref)), split(rows_of(v_ref))]
    base = rows_of(e_ref)
    for k in range(2):
        at = slice(k * NB, (k + 1) * NB)
        base = base - dot3(left[k], (h_ref[at, :], l_ref[at, :]))
    finished = lax.broadcasted_iota(jnp.int32, base.shape, 0) < 512
    base = jnp.where(finished & (r_ref[0] == 0) & (step == 0), 0.0, base)
    put_rows(base_ref, base)

    @pl.when((r_ref[0] == 0) & (step == 0))
    def _():
        gram_ref[NB:, :] = base[512 : 512 + NB]

    turned = base.T
    parts = split(turned)
    gram_ref[:NB, :] += nn(turned, base)
    for k in range(2):
        turn_ref[:, k * NB : (k + 1) * NB] += dot3(parts, left[k])
    acc_ref[...] += dot3(parts, split(m_ref[...]))

    @pl.when(step == pl.num_programs(0) - 1)
    def _():
        prod_ref[...] = acc_ref[...].T
        cross_ref[...] = turn_ref[...].T


def second_of(row, cols, image, vectors, right, matrix):
    high, low = split_outside(right)
    base, gram, cross, product = pl.pallas_call(
        second_kernel,
        grid=(4,),
        in_specs=[
            pl.BlockSpec(memory_space=pltpu.SMEM),
            GATHERED,
            GATHERED,
            GATHERED,
            whole((2 * NB, NB)),
            whole((2 * NB, NB)),
            NATURAL,
        ],
        out_specs=[GATHERED] + [whole((512, NB))] * 3,
        out_shape=[
            GATHERED_SHAPE,
            *[jax.ShapeDtypeStruct((512, NB), F32)] * 3,
        ],
        scratch_shapes=[pltpu.VMEM((NB, 512), F32)] * 2,
        compiler_params=LARGE,
        cost_estimate=cost(18),
        name="second",
    )(row[None], blocks_of(cols), blocks_of(image), blocks_of(vectors), high, low, matrix)
    return base.reshape(4096, NB), gram, cross, product


def update_kernel(m_ref, r_ref, *refs):
    parts = [split(rows_of(ref)) for ref in refs[:-1]]
    tops = [top for top, _ in parts]
    left = jnp.concatenate(tops + tops + [rest for _, rest in parts], 1)
    refs[-1][...] = m_ref[...] - jnp.dot(left, r_ref[...], preferred_element_type=F32)


def update_of(matrix, lefts, right):
    top, rest = split_outside(right)
    stack = jnp.concatenate([top, rest, top], 0)
    return pl.pallas_call(
        update_kernel,
        grid=(4,),
        in_specs=[NATURAL, whole(stack.shape)] + [GATHERED] * len(lefts),
        out_specs=NATURAL,
        out_shape=jax.ShapeDtypeStruct((4096, 512), F32),
        compiler_params=LARGE,
        cost_estimate=cost(7 + 3 * len(lefts)),
        name="update",
    )(matrix, stack, *(blocks_of(left) for left in lefts))


def diagonal_inverse(block, size):
    rows = lax.broadcasted_iota(jnp.int32, (size, 128), 0)
    lanes = lax.broadcasted_iota(jnp.int32, (size, 128), 1)
    work = jnp.where(lanes < size, block, (lanes - size == rows).astype(F32))
    count = size // 8
    groups = [work[8 * i : 8 * i + 8] for i in range(count)]
    place = rows[:8]

    def spread(tile, t):
        return jnp.broadcast_to(tile[t : t + 1, :], (8, 128))

    for a in range(count):
        columns = [
            [jnp.broadcast_to(groups[i][:, k : k + 1], (8, 128)) for k in range(8 * a, 8 * a + 8)]
            for i in range(a, count)
        ]
        for t in range(8):
            if a == count - 1 and t == 7:
                break
            scale = 1.0 / spread(columns[0][t], t)
            row = spread(groups[a], t)
            heads = [spread(columns[0][u], t) for u in range(t + 1, 8)]
            for i in range(a, count):
                own = columns[i - a]
                factor = own[t] * scale
                if i == a:
                    if t == 7:
                        continue
                    factor = jnp.where(place > t, factor, 0.0)
                groups[i] = groups[i] - factor * row
                for u in range(t + 1, 8):
                    own[u] = own[u] - factor * heads[u - t - 1]
    work = jnp.concatenate(groups, 0)
    diag = jnp.sum(jnp.where(lanes == rows, work, 0.0), axis=1, keepdims=True)
    return (work / jnp.sqrt(diag))[:, size : 2 * size]


def invert_factor(m_ref, x_ref, size=64):
    rows = lax.broadcasted_iota(jnp.int32, (NB, NB), 0)
    x_ref[...] = (rows == lax.broadcasted_iota(jnp.int32, (NB, NB), 1)).astype(F32)
    lane = lax.broadcasted_iota(jnp.int32, (size, NB), 1)
    for at in range(0, NB, size):
        strip = m_ref[at : at + size, :]
        block = strip[:, at // 128 * 128 : at // 128 * 128 + 128]
        if at % 128:
            block = pltpu.roll(block, 128 - at % 128, 1)
        inv = diagonal_inverse(block, size)
        strip = jnp.where(lane >= at, nn(inv, strip), 0.0)
        solved = nn(inv, x_ref[at : at + size, :])
        below = at + size
        if below < NB:
            left = strip.T[below:]
            m_ref[below:, :] -= nn(left, strip)
            x_ref[below:, :] -= nn(left, solved)
        x_ref[at : at + size, :] = solved


def factor_kernel(g_ref, inv_ref, m_ref):
    m_ref[...] = g_ref[...]
    invert_factor(m_ref, inv_ref)


def inverse_factor(gram):
    return pl.pallas_call(
        factor_kernel,
        out_shape=SQUARE,
        scratch_shapes=[pltpu.VMEM((NB, NB), F32)],
        cost_estimate=cost(12),
        name="factor",
    )(gram)


def coupling_kernel(t_ref, inv_ref, top_ref, out_ref, m_ref, f_ref):
    rows = lax.broadcasted_iota(jnp.int32, (NB, NB), 0)
    eye = (rows == lax.broadcasted_iota(jnp.int32, (NB, NB), 1)).astype(F32)
    top = eye - nt(t_ref[...], inv_ref[...])
    top_ref[...] = top
    m_ref[...] = nt(top, top)
    invert_factor(m_ref, f_ref)
    factor = f_ref[...]
    out_ref[...] = nn(factor.T, nn(factor, top))


def coupling_of(base_top, inv):
    return pl.pallas_call(
        coupling_kernel,
        out_shape=(SQUARE, SQUARE),
        scratch_shapes=[pltpu.VMEM((NB, NB), F32)] * 2,
        cost_estimate=cost(14),
        name="coupling",
    )(base_top, inv)


def shards(matrix):
    z, y, xh = (lax.axis_index(a) for a in COL)
    row = lax.axis_index(ROW)
    on_first = row == 0
    lanes = jnp.arange(NB, dtype=jnp.int32)[None, :]

    where_in = jnp.arange(32 * PIECE, dtype=jnp.int32)
    gathered_rows = (
        row * 4096
        + (where_in // 256 % 4 * 2 + where_in // 128 % 2) * 512
        + where_in // 1024 * 128
        + where_in % 128
    )[:, None]
    column_rows = (((z * 4 + y) * 2 + xh) * 512 + jnp.arange(512, dtype=jnp.int32))[:, None]
    piece_rows = (
        row * 4096 + (y * 2 + xh) * 512 + z * 128 + jnp.arange(128, dtype=jnp.int32)
    )[:, None]

    def unit(rows, first):
        return (rows - first == lanes).astype(F32)

    def rows_at(block, first):
        cube = block.reshape(4, 8, PIECE, NB)
        at = first // 512
        q = first % 512 // 128
        return jnp.where(on_first, jnp.concatenate([cube[q, at], cube[q + 1, at]], 0), 0.0)

    def high(dims, left, right):
        return contract(left, right, dims, lax.Precision.HIGH)

    wide_nt, wide_nn = ((1,), (1,)), ((1,), (0,))

    strip = core_half(jnp.where(on_first, matrix[: 3 * NB].T, 0.0))
    pieces = scatter_pieces(strip[:, : 2 * NB])
    base_piece, next_piece = jnp.where(piece_rows >= NB, pieces[:, :NB], 0.0), pieces[:, NB:]
    next_cols = lax.all_gather(next_piece, COL, tiled=True)
    base = gather_rows(pair_up(base_piece))

    partial, gram = product_of(matrix, base)
    half = core_half(partial)
    product_p = piece_of(half)
    stat = jnp.concatenate([gram, rows_at(base, 256), rows_at(base, 512)], 0)
    product_p, stat, half = lax.optimization_barrier((product_p, stat, half))
    pair, next_cols = lax.optimization_barrier((pair_up(product_p), next_cols))
    product = gather_pairs(pair)
    stat = row_sum(stat)
    product_j = both_halves(half + swap(half, "xl"))
    stat, strip = lax.optimization_barrier((stat, strip))
    inv, last_piece, link = lax.optimization_barrier(
        (inverse_factor(stat[:256]), scatter_pieces(strip[:, 2 * NB :]), swap(strip, "xl"))
    )
    strip = both_halves(strip + link)
    vectors = unit(gathered_rows, 256) - high(wide_nt, base, inv)
    def side(rows, base_rows, first_rows, prod):
        return (
            unit(rows, 256) - high(wide_nt, base_rows, inv),
            first_rows - high(wide_nt, prod, inv),
        )

    product, vectors_p, image_p = lax.optimization_barrier(
        (product, *side(piece_rows, base_piece, next_piece, product_p))
    )
    image, inner = image_of(next_cols, product, vectors, inv)
    base_tops = stat[256:]
    stat = core_half(jnp.concatenate([inner, rows_at(image, 256), rows_at(image, 512)], 0))
    stat, base_tops = lax.optimization_barrier((stat, base_tops))
    top_next = -nt(base_tops[256:], inv)
    link, (top, coupling) = lax.optimization_barrier(
        (swap(stat, "xl"), coupling_of(base_tops[:256], inv))
    )
    stat = both_halves(stat + link)
    inner = nn(tn(coupling, stat[:256]), coupling)
    image_top, image_next = stat[256:512], stat[512:]

    def factors(vec, img):
        return nt(coupling, vec), tn(coupling, img.T) - nt(inner, vec)

    right = jnp.concatenate(factors(top, image_top), 0)
    base2, gram, cross, partial = second_of(row, next_cols, image, vectors, right, matrix)
    stat, half, cross, image_next, strip = lax.optimization_barrier(
        (core_half(gram), core_half(partial), core_half(cross), image_next, strip)
    )
    next_a, next_b = factors(top_next, image_next)
    cols_p = last_piece - high(wide_nn, image_p, next_a) - high(wide_nn, vectors_p, next_b)
    first_j = strip[:, 256:512]
    vectors_j, image_j = side(
        column_rows, jnp.where(column_rows >= 256, strip[:, :256], 0.0), first_j, product_j
    )
    cols_j = strip[:, 512:] - high(wide_nn, image_j, next_a) - high(wide_nn, vectors_j, next_b)
    base2_j = jnp.where(
        column_rows >= 512,
        first_j - high(wide_nn, image_j, right[:256]) - high(wide_nn, vectors_j, right[256:]),
        0.0,
    )
    stat, half, cross, cols_p, cols_j, base2_j = lax.optimization_barrier(
        (stat + swap(stat, "xl"), half, cross, cols_p, cols_j, base2_j)
    )
    stat = both_halves(stat)
    product_p2, product_j2, cross = piece_of(half), half + swap(half, "xl"), cross + swap(cross, "xl")
    inv2, product_p2, product_j2, cross = lax.optimization_barrier(
        (inverse_factor(stat[:256]), product_p2, product_j2, cross)
    )
    product_j2, cross = both_halves(product_j2), both_halves(cross)
    mix_v = tn(coupling, cross[:256]) - nn(inner, cross[256:])
    mix_i = nn(coupling, cross[256:])

    def second_image(cols, vec, img, prod):
        prod = prod - high(wide_nn, vec, mix_v) - high(wide_nn, img, mix_i)
        return cols - high(wide_nt, prod, inv2)

    image2 = gather_pairs(pair_up(second_image(cols_p, vectors_p, image_p, product_p2)))
    image2_j = second_image(cols_j, vectors_j, image_j, product_j2)
    vectors2_j = unit(column_rows, 512) - high(wide_nt, base2_j, inv2)

    part = lax.dynamic_slice_in_dim(tn(vectors2_j, image2_j), row * 64, 64, 0)
    part = part + swap(part, "xh")
    part, (top2, coupling2) = lax.optimization_barrier((part, coupling_of(stat[256:], inv2)))
    part = axis_sum(part, "y")
    vectors2 = unit(gathered_rows, 512) - high(wide_nt, base2, inv2)
    part, vectors2 = lax.optimization_barrier((part, vectors2))
    inner2 = lax.all_gather(axis_sum(part, "z"), ROW, tiled=True)
    inner2 = nn(tn(coupling2, inner2), coupling2)
    last_a = nt(coupling2, vectors2_j)
    last_b = tn(coupling2, image2_j.T) - nt(inner2, vectors2_j)
    first_a, first_b = factors(vectors_j, image_j)
    right = jnp.concatenate([first_a, first_b, last_b, last_a], 0)
    return update_of(matrix, (image, vectors, vectors2, image2), right)


def solution(mesh):
    fine = Mesh(mesh.devices.reshape(4, 4, 2, 2, 2), COL + ROW)
    return jax.shard_map(
        shards,
        mesh=fine,
        in_specs=(P(ROW, COL),),
        out_specs=P(ROW, COL),
        check_vma=False,
    )
```

```python
import jax
import jax.numpy as jnp
from jax import lax
from jax.experimental import pallas as pl
from jax.experimental.pallas import tpu as pltpu
from jax.sharding import Mesh, PartitionSpec as P

NB = 256
PIECE = 128
COL = ("z", "y", "xh")
ROW = ("xl", "c")
F32 = jnp.float32


def contract(left, right, dims, precision=lax.Precision.HIGHEST):
    return lax.dot_general(
        left, right, (dims, ((), ())), precision=precision, preferred_element_type=F32
    )


def nn(left, right):
    return contract(left, right, ((1,), (0,)))


def tn(left, right):
    return contract(left, right, ((0,), (0,)))


def nt(left, right):
    return contract(left, right, ((1,), (1,)))


def ring(block, axis, shift):
    return lax.ppermute(block, axis, [(k, (k + shift) % 4) for k in range(4)])


def swap(block, axis):
    return lax.ppermute(block, axis, [(0, 1), (1, 0)])


def core_half(stacked):
    half = stacked.shape[0] // 2
    core = lax.axis_index("c")
    low, high = stacked[:half], stacked[half:]
    return jnp.where(core == 0, low, high) + swap(jnp.where(core == 0, high, low), "c")


def both_halves(mine):
    core = lax.axis_index("c")
    other = swap(mine, "c")
    return jnp.concatenate(
        [jnp.where(core == 0, mine, other), jnp.where(core == 0, other, mine)], 0
    )


def row_sum(stacked):
    mine = core_half(stacked)
    return both_halves(mine + swap(mine, "xl"))


def gather_rows(pair):
    z, y = lax.axis_index("z"), lax.axis_index("y")
    out = jnp.zeros((4, 4, 2 * PIECE, NB), F32)
    for half, (first, second) in enumerate((("y", "z"), ("z", "y"))):
        at_first, at_second = (y, z) if half == 0 else (z, y)
        own = pair[:, half * 128 : (half + 1) * 128]
        left, right, far = ring(own, first, 1), ring(own, first, 3), ring(own, first, 2)
        line = jnp.zeros((4, 2 * PIECE, 128), F32)
        for shift, block in ((0, own), (-1, left), (1, right), (2, far)):
            line = lax.dynamic_update_slice(line, block[None], ((at_first + shift) % 4, 0, 0))
        left, right = ring(line, second, 1), ring(line, second, 3)
        far = jnp.concatenate([ring(left[:2], second, 1), ring(right[2:], second, 3)], 0)
        for shift, block in ((0, line), (-1, left), (1, right), (2, far)):
            place = (at_second + shift) % 4
            if half == 0:
                out = lax.dynamic_update_slice(out, block[None], (place, 0, 0, 0))
            else:
                out = lax.dynamic_update_slice(out, block[:, None], (0, place, 0, 128))
    return out.reshape(32 * PIECE, NB)


def piece_of(mine):
    xl = lax.axis_index("xl")
    piece = 0.0
    for k in range(2):
        part = lax.dynamic_slice_in_dim(mine, ((xl + k) % 2) * PIECE, PIECE, 0)
        perm = [
            ((z * 2 + l) * 2 + c, (2 * c + (l + k) % 2) * 4 + z)
            for z in range(4)
            for l in range(2)
            for c in range(2)
        ]
        piece = piece + lax.ppermute(part, ("z", "xl", "c"), perm)
    return piece


def scatter_pieces(half):
    piece = 0.0
    for k in range(2):
        perm = [(z * 4 + c, (2 * c + k) * 4 + z) for z in range(4) for c in range(2)]
        piece = piece + lax.ppermute(
            half[k * PIECE : (k + 1) * PIECE], ("z", "xl", "c"), perm
        )
    return piece


def pair_up(piece):
    xh = lax.axis_index("xh")
    other = swap(piece, "xh")
    return jnp.concatenate(
        [jnp.where(xh == 0, piece, other), jnp.where(xh == 0, other, piece)], 0
    )


def gather_pairs(pair):
    return lax.all_gather(pair, ("z", "y"), tiled=True)


def axis_sum(block, axis):
    return (block + ring(block, axis, 2)) + (ring(block, axis, 1) + ring(block, axis, 3))


BF16 = jnp.bfloat16


def split(block):
    high = block.astype(BF16)
    return high, (block - high.astype(F32)).astype(BF16)


def split_outside(block):
    high = lax.reduce_precision(block, 8, 7)
    return high.astype(BF16), (block - high).astype(BF16)


def dot3(left, right):
    (lh, ll), (rh, rl) = left, right

    def dot(a, b):
        return jnp.dot(a, b, preferred_element_type=F32)

    return dot(lh, rh) + (dot(lh, rl) + dot(ll, rh))


def whole(shape):
    return pl.BlockSpec(shape, lambda b: (0,) * len(shape))


NATURAL = pl.BlockSpec((1024, 512), lambda b: (b, 0))
GATHERED = pl.BlockSpec((4, 2, PIECE, NB), lambda b: (0, b, 0, 0))
GATHERED_SHAPE = jax.ShapeDtypeStruct((4, 8, PIECE, NB), F32)
SQUARE = jax.ShapeDtypeStruct((NB, NB), F32)
LARGE = pltpu.CompilerParams(vmem_limit_bytes=48 << 20)


def cost(us):
    return pl.CostEstimate(flops=us * 10**9, bytes_accessed=us << 20, transcendentals=0)


def rows_of(ref):
    return jnp.concatenate([ref[:, k].reshape(512, NB) for k in range(2)], 0)


def put_rows(ref, rows):
    for k in range(2):
        ref[:, k] = rows[k * 512 : (k + 1) * 512].reshape(4, PIECE, NB)


def blocks_of(array):
    return array.reshape(4, 8, PIECE, NB)


def product_kernel(m_ref, b_ref, out_ref, gram_ref, acc_ref):
    step = pl.program_id(0)

    @pl.when(step == 0)
    def _():
        acc_ref[...] = jnp.zeros_like(acc_ref)
        gram_ref[...] = jnp.zeros_like(gram_ref)

    base = rows_of(b_ref)
    turned = base.T
    acc_ref[...] += dot3(split(turned), split(m_ref[...]))
    gram_ref[...] += nn(turned, base)

    @pl.when(step == pl.num_programs(0) - 1)
    def _():
        out_ref[...] = acc_ref[...].T


def product_of(matrix, base):
    return pl.pallas_call(
        product_kernel,
        grid=(4,),
        in_specs=[NATURAL, GATHERED],
        out_specs=[whole((512, NB)), whole((NB, NB))],
        out_shape=[jax.ShapeDtypeStruct((512, NB), F32), SQUARE],
        scratch_shapes=[pltpu.VMEM((NB, 512), F32)],
        compiler_params=LARGE,
        cost_estimate=cost(13),
        name="product",
    )(matrix, blocks_of(base))


def image_kernel(e_ref, w_ref, v_ref, h_ref, l_ref, out_ref, inner_ref):
    step = pl.program_id(0)

    @pl.when(step == 0)
    def _():
        inner_ref[...] = jnp.zeros_like(inner_ref)

    image = rows_of(e_ref) - dot3(split(rows_of(w_ref)), (h_ref[...], l_ref[...]))
    put_rows(out_ref, image)
    inner_ref[...] += dot3(split(image.T), split(rows_of(v_ref)))


def image_of(cols, product, vectors, inv):
    high, low = split_outside(inv.T)
    image, inner = pl.pallas_call(
        image_kernel,
        grid=(4,),
        in_specs=[GATHERED, GATHERED, GATHERED, whole((NB, NB)), whole((NB, NB))],
        out_specs=[GATHERED, whole((NB, NB))],
        out_shape=[GATHERED_SHAPE, SQUARE],
        compiler_params=LARGE,
        cost_estimate=cost(11),
        name="image",
    )(blocks_of(cols), blocks_of(product), blocks_of(vectors), high, low)
    return image.reshape(4096, NB), inner


def second_kernel(r_ref, e_ref, i_ref, v_ref, h_ref, l_ref, m_ref, base_ref, gram_ref, cross_ref, prod_ref, acc_ref, turn_ref):
    step = pl.program_id(0)

    @pl.when(step == 0)
    def _():
        gram_ref[...] = jnp.zeros_like(gram_ref)
        turn_ref[...] = jnp.zeros_like(turn_ref)
        acc_ref[...] = jnp.zeros_like(acc_ref)

    left = [split(rows_of(i_ref)), split(rows_of(v_ref))]
    base = rows_of(e_ref)
    for k in range(2):
        at = slice(k * NB, (k + 1) * NB)
        base = base - dot3(left[k], (h_ref[at, :], l_ref[at, :]))
    finished = lax.broadcasted_iota(jnp.int32, base.shape, 0) < 512
    base = jnp.where(finished & (r_ref[0] == 0) & (step == 0), 0.0, base)
    put_rows(base_ref, base)

    @pl.when((r_ref[0] == 0) & (step == 0))
    def _():
        gram_ref[NB:, :] = base[512 : 512 + NB]

    turned = base.T
    parts = split(turned)
    gram_ref[:NB, :] += nn(turned, base)
    for k in range(2):
        turn_ref[:, k * NB : (k + 1) * NB] += dot3(parts, left[k])
    acc_ref[...] += dot3(parts, split(m_ref[...]))

    @pl.when(step == pl.num_programs(0) - 1)
    def _():
        prod_ref[...] = acc_ref[...].T
        cross_ref[...] = turn_ref[...].T


def second_of(row, cols, image, vectors, right, matrix):
    high, low = split_outside(right)
    base, gram, cross, product = pl.pallas_call(
        second_kernel,
        grid=(4,),
        in_specs=[
            pl.BlockSpec(memory_space=pltpu.SMEM),
            GATHERED,
            GATHERED,
            GATHERED,
            whole((2 * NB, NB)),
            whole((2 * NB, NB)),
            NATURAL,
        ],
        out_specs=[GATHERED] + [whole((512, NB))] * 3,
        out_shape=[
            GATHERED_SHAPE,
            *[jax.ShapeDtypeStruct((512, NB), F32)] * 3,
        ],
        scratch_shapes=[pltpu.VMEM((NB, 512), F32)] * 2,
        compiler_params=LARGE,
        cost_estimate=cost(18),
        name="second",
    )(row[None], blocks_of(cols), blocks_of(image), blocks_of(vectors), high, low, matrix)
    return base.reshape(4096, NB), gram, cross, product


def update_kernel(m_ref, r_ref, *refs):
    parts = [split(rows_of(ref)) for ref in refs[:-1]]
    tops = [top for top, _ in parts]
    left = jnp.concatenate(tops + tops + [rest for _, rest in parts], 1)
    refs[-1][...] = m_ref[...] - jnp.dot(left, r_ref[...], preferred_element_type=F32)


def update_of(matrix, lefts, right):
    top, rest = split_outside(right)
    stack = jnp.concatenate([top, rest, top], 0)
    return pl.pallas_call(
        update_kernel,
        grid=(4,),
        in_specs=[NATURAL, whole(stack.shape)] + [GATHERED] * len(lefts),
        out_specs=NATURAL,
        out_shape=jax.ShapeDtypeStruct((4096, 512), F32),
        compiler_params=LARGE,
        cost_estimate=cost(7 + 3 * len(lefts)),
        name="update",
    )(matrix, stack, *(blocks_of(left) for left in lefts))


def diagonal_inverse(block, size):
    rows = lax.broadcasted_iota(jnp.int32, (size, 128), 0)
    lanes = lax.broadcasted_iota(jnp.int32, (size, 128), 1)
    work = jnp.where(lanes < size, block, (lanes - size == rows).astype(F32))
    count = size // 8
    groups = [work[8 * i : 8 * i + 8] for i in range(count)]
    place = rows[:8]

    def spread(tile, t):
        return jnp.broadcast_to(tile[t : t + 1, :], (8, 128))

    for a in range(count):
        columns = [
            [jnp.broadcast_to(groups[i][:, k : k + 1], (8, 128)) for k in range(8 * a, 8 * a + 8)]
            for i in range(a, count)
        ]
        for t in range(8):
            if a == count - 1 and t == 7:
                break
            scale = 1.0 / spread(columns[0][t], t)
            row = spread(groups[a], t)
            heads = [spread(columns[0][u], t) for u in range(t + 1, 8)]
            for i in range(a, count):
                own = columns[i - a]
                factor = own[t] * scale
                if i == a:
                    if t == 7:
                        continue
                    factor = jnp.where(place > t, factor, 0.0)
                groups[i] = groups[i] - factor * row
                for u in range(t + 1, 8):
                    own[u] = own[u] - factor * heads[u - t - 1]
    work = jnp.concatenate(groups, 0)
    diag = jnp.sum(jnp.where(lanes == rows, work, 0.0), axis=1, keepdims=True)
    return (work / jnp.sqrt(diag))[:, size : 2 * size]


def invert_factor(m_ref, x_ref, size=64):
    rows = lax.broadcasted_iota(jnp.int32, (NB, NB), 0)
    x_ref[...] = (rows == lax.broadcasted_iota(jnp.int32, (NB, NB), 1)).astype(F32)
    lane = lax.broadcasted_iota(jnp.int32, (size, NB), 1)
    for at in range(0, NB, size):
        strip = m_ref[at : at + size, :]
        block = strip[:, at // 128 * 128 : at // 128 * 128 + 128]
        if at % 128:
            block = pltpu.roll(block, 128 - at % 128, 1)
        inv = diagonal_inverse(block, size)
        strip = jnp.where(lane >= at, nn(inv, strip), 0.0)
        solved = nn(inv, x_ref[at : at + size, :])
        below = at + size
        if below < NB:
            left = strip.T[below:]
            m_ref[below:, :] -= nn(left, strip)
            x_ref[below:, :] -= nn(left, solved)
        x_ref[at : at + size, :] = solved


def factor_kernel(g_ref, inv_ref, m_ref):
    m_ref[...] = g_ref[...]
    invert_factor(m_ref, inv_ref)


def inverse_factor(gram):
    return pl.pallas_call(
        factor_kernel,
        out_shape=SQUARE,
        scratch_shapes=[pltpu.VMEM((NB, NB), F32)],
        cost_estimate=cost(12),
        name="factor",
    )(gram)


def coupling_kernel(t_ref, inv_ref, top_ref, out_ref, m_ref, f_ref):
    rows = lax.broadcasted_iota(jnp.int32, (NB, NB), 0)
    eye = (rows == lax.broadcasted_iota(jnp.int32, (NB, NB), 1)).astype(F32)
    top = eye - nt(t_ref[...], inv_ref[...])
    top_ref[...] = top
    m_ref[...] = nt(top, top)
    invert_factor(m_ref, f_ref)
    factor = f_ref[...]
    out_ref[...] = nn(factor.T, nn(factor, top))


def coupling_of(base_top, inv):
    return pl.pallas_call(
        coupling_kernel,
        out_shape=(SQUARE, SQUARE),
        scratch_shapes=[pltpu.VMEM((NB, NB), F32)] * 2,
        cost_estimate=cost(14),
        name="coupling",
    )(base_top, inv)


def shards(matrix):
    z, y, xh = (lax.axis_index(a) for a in COL)
    row = lax.axis_index(ROW)
    on_first = row == 0
    lanes = jnp.arange(NB, dtype=jnp.int32)[None, :]

    where_in = jnp.arange(32 * PIECE, dtype=jnp.int32)
    gathered_rows = (
        row * 4096
        + (where_in // 256 % 4 * 2 + where_in // 128 % 2) * 512
        + where_in // 1024 * 128
        + where_in % 128
    )[:, None]
    column_rows = (((z * 4 + y) * 2 + xh) * 512 + jnp.arange(512, dtype=jnp.int32))[:, None]
    piece_rows = (
        row * 4096 + (y * 2 + xh) * 512 + z * 128 + jnp.arange(128, dtype=jnp.int32)
    )[:, None]

    def unit(rows, first):
        return (rows - first == lanes).astype(F32)

    def rows_at(block, first):
        cube = block.reshape(4, 8, PIECE, NB)
        at = first // 512
        q = first % 512 // 128
        return jnp.where(on_first, jnp.concatenate([cube[q, at], cube[q + 1, at]], 0), 0.0)

    def high(dims, left, right):
        return contract(left, right, dims, lax.Precision.HIGH)

    wide_nt, wide_nn = ((1,), (1,)), ((1,), (0,))

    def nn(left, right):
        return high(wide_nn, left, right)

    def tn(left, right):
        return high(((0,), (0,)), left, right)

    def nt(left, right):
        return high(wide_nt, left, right)

    strip = core_half(jnp.where(on_first, matrix[: 3 * NB].T, 0.0))
    pieces = scatter_pieces(strip[:, : 2 * NB])
    base_piece, next_piece = jnp.where(piece_rows >= NB, pieces[:, :NB], 0.0), pieces[:, NB:]
    next_cols = lax.all_gather(next_piece, COL, tiled=True)
    base = gather_rows(pair_up(base_piece))

    partial, gram = product_of(matrix, base)
    half = core_half(partial)
    product_p = piece_of(half)
    stat = jnp.concatenate([gram, rows_at(base, 256), rows_at(base, 512)], 0)
    product_p, stat, half = lax.optimization_barrier((product_p, stat, half))
    pair, next_cols = lax.optimization_barrier((pair_up(product_p), next_cols))
    product = gather_pairs(pair)
    stat = row_sum(stat)
    product_j = both_halves(half + swap(half, "xl"))
    stat, strip = lax.optimization_barrier((stat, strip))
    inv, last_piece, link = lax.optimization_barrier(
        (inverse_factor(stat[:256]), scatter_pieces(strip[:, 2 * NB :]), swap(strip, "xl"))
    )
    strip = both_halves(strip + link)
    vectors = unit(gathered_rows, 256) - high(wide_nt, base, inv)
    def side(rows, base_rows, first_rows, prod):
        return (
            unit(rows, 256) - high(wide_nt, base_rows, inv),
            first_rows - high(wide_nt, prod, inv),
        )

    product, vectors_p, image_p = lax.optimization_barrier(
        (product, *side(piece_rows, base_piece, next_piece, product_p))
    )
    image, inner = image_of(next_cols, product, vectors, inv)
    base_tops = stat[256:]
    stat = core_half(jnp.concatenate([inner, rows_at(image, 256), rows_at(image, 512)], 0))
    stat, base_tops = lax.optimization_barrier((stat, base_tops))
    top_next = -nt(base_tops[256:], inv)
    link, (top, coupling) = lax.optimization_barrier(
        (swap(stat, "xl"), coupling_of(base_tops[:256], inv))
    )
    stat = both_halves(stat + link)
    inner = nn(tn(coupling, stat[:256]), coupling)
    image_top, image_next = stat[256:512], stat[512:]

    def factors(vec, img):
        return nt(coupling, vec), tn(coupling, img.T) - nt(inner, vec)

    right = jnp.concatenate(factors(top, image_top), 0)
    base2, gram, cross, partial = second_of(row, next_cols, image, vectors, right, matrix)
    stat, half, cross, image_next, strip = lax.optimization_barrier(
        (core_half(gram), core_half(partial), core_half(cross), image_next, strip)
    )
    next_a, next_b = factors(top_next, image_next)
    cols_p = last_piece - high(wide_nn, image_p, next_a) - high(wide_nn, vectors_p, next_b)
    first_j = strip[:, 256:512]
    vectors_j, image_j = side(
        column_rows, jnp.where(column_rows >= 256, strip[:, :256], 0.0), first_j, product_j
    )
    cols_j = strip[:, 512:] - high(wide_nn, image_j, next_a) - high(wide_nn, vectors_j, next_b)
    base2_j = jnp.where(
        column_rows >= 512,
        first_j - high(wide_nn, image_j, right[:256]) - high(wide_nn, vectors_j, right[256:]),
        0.0,
    )
    stat, half, cross, cols_p, cols_j, base2_j = lax.optimization_barrier(
        (stat + swap(stat, "xl"), half, cross, cols_p, cols_j, base2_j)
    )
    stat = both_halves(stat)
    product_p2, product_j2, cross = piece_of(half), half + swap(half, "xl"), cross + swap(cross, "xl")
    inv2, product_p2, product_j2, cross = lax.optimization_barrier(
        (inverse_factor(stat[:256]), product_p2, product_j2, cross)
    )
    product_j2, cross = both_halves(product_j2), both_halves(cross)
    mix_v = tn(coupling, cross[:256]) - nn(inner, cross[256:])
    mix_i = nn(coupling, cross[256:])

    def second_image(cols, vec, img, prod):
        prod = prod - high(wide_nn, vec, mix_v) - high(wide_nn, img, mix_i)
        return cols - high(wide_nt, prod, inv2)

    image2 = gather_pairs(pair_up(second_image(cols_p, vectors_p, image_p, product_p2)))
    image2_j = second_image(cols_j, vectors_j, image_j, product_j2)
    vectors2_j = unit(column_rows, 512) - high(wide_nt, base2_j, inv2)

    part = lax.dynamic_slice_in_dim(tn(vectors2_j, image2_j), row * 64, 64, 0)
    part = part + swap(part, "xh")
    part, (top2, coupling2) = lax.optimization_barrier((part, coupling_of(stat[256:], inv2)))
    part = axis_sum(part, "y")
    vectors2 = unit(gathered_rows, 512) - high(wide_nt, base2, inv2)
    part, vectors2 = lax.optimization_barrier((part, vectors2))
    inner2 = lax.all_gather(axis_sum(part, "z"), ROW, tiled=True)
    inner2 = nn(tn(coupling2, inner2), coupling2)
    last_a = nt(coupling2, vectors2_j)
    last_b = tn(coupling2, image2_j.T) - nt(inner2, vectors2_j)
    first_a, first_b = factors(vectors_j, image_j)
    right = jnp.concatenate([first_a, first_b, last_b, last_a], 0)
    return update_of(matrix, (image, vectors, vectors2, image2), right)


def solution(mesh):
    fine = Mesh(mesh.devices.reshape(4, 4, 2, 2, 2), COL + ROW)
    return jax.shard_map(
        shards,
        mesh=fine,
        in_specs=(P(ROW, COL),),
        out_specs=P(ROW, COL),
        check_vma=False,
    )
```
